128 devices in a mesh: gx: 16 (over x, y_hi, core), gy: 8 (over y_lo, z).
Axes of the slice: x: 4, y: 4 (y_hi: 2, y_lo: 2; y = y_hi * 2 + y_lo), z: 4, core: 2. Of those that a mesh axis runs over, the one named last changes fastest.
Arguments:
- right_side: float32 [512, 256, 512], P('gx', 'gy'), may hold values from -24 to 24
- alpha_coef: float32 [512, 256, 512], P('gx', 'gy'), may hold values from 0.05 to 0.5
- face_coef: float32 [3, 512, 256, 512], P(None, 'gx', 'gy'), may hold values from 0.25 to 4
- owner_map: int32 [8, 256], P('gy'), may hold values from 0 to 15, as said below
Outputs:
- solution: float32 [512, 256, 512], P('gx', 'gy')
- coarse_residual: float32 [256, 128, 256], P('gx', 'gy')
- coarse_coef: float32 [4, 256, 128, 256], P(None, 'gx', 'gy')
The draws below stay inside these ranges and needn't reach their ends.
Inputs may be any that keep to these rules, and one draw needn't show every extreme that they name: `owner_map`: each row's tiles are cut by recursive bisection into boxes of 4 x 4 tiles, one box to each owner; every device that sends to an owner sends it exactly 4 tiles.
All inputs are finite; a program needn't handle non-finite values.
Results may differ from the reference program's by a relative error of at most 0.00002.
Values sent between devices are 32-bit elements; how exact they have to be, the bound alone decides.
A program may use at most 192 MiB of HBM per device.

```python
import math
import jax
import jax.numpy as jnp

SIDE = 4
ITERS = 4
TZ = 16
HALF = 16
NX = 512
NY = 256
NZ = 512
TILES = 256
N_GX = 16
N_GY = 8


def draw_owner_map(key, part):
    boxes_x = N_GX // SIDE
    extent_x = boxes_x
    extent_z = SIDE
    levels = []
    while extent_x * extent_z > 1:
        if extent_x >= extent_z:
            extent_x = extent_x // 2
            levels.append((0, extent_x))
        else:
            extent_z = extent_z // 2
            levels.append((1, extent_z))
    box_x = jnp.broadcast_to((jnp.arange(N_GX, dtype=jnp.int32) // SIDE)[:, None], (N_GX, TZ))
    box_z = jnp.broadcast_to((jnp.arange(TZ, dtype=jnp.int32) // SIDE)[None, :], (N_GX, TZ))
    label = jnp.zeros((N_GY, N_GX * TZ), jnp.int32)
    node_id = jnp.zeros((N_GY, N_GX * TZ), jnp.int32)
    for level_index, (split_dim, split_size) in enumerate(levels):
        coords = box_x if split_dim == 0 else box_z
        half_bit = (coords // split_size % 2).reshape(1, N_GX * TZ)
        flips = jax.random.randint(jax.random.fold_in(key, level_index + 11), (N_GY, 2 ** level_index), 0, 2).astype(jnp.int32)
        flip_bit = jnp.take_along_axis(flips, node_id, axis=1)
        label = label * 2 + (half_bit + flip_bit) % 2
        node_id = node_id * 2 + half_bit
    return label.astype(jnp.int32)


def block_levels(rng, shape, pieces, least, largest):
    def one(axis_at, parts):
        steps = jax.random.uniform(jax.random.fold_in(jax.random.fold_in(rng, 6), axis_at), (parts,), jnp.float32, least / len(pieces), largest / len(pieces))
        return jnp.repeat(jnp.exp(steps), shape[axis_at] // parts).reshape((-1,) + (1,) * (len(shape) - axis_at - 1))

    loudness = one(*pieces[0])
    for cut in pieces[1:]:
        loudness = loudness * one(*cut)
    return loudness


def scatter_about(rng, shape, scale, limit, shards=(), kind=jnp.bfloat16):
    entries = scale * jax.random.normal(rng, shape, jnp.float32)
    if shards:
        entries = entries * block_levels(rng, shape, shards, -0.22, 0.18)
    return jnp.clip(entries, -limit, limit).astype(kind)


def setup_inputs(seed: int = 0) -> dict:
    splits = jax.random.split(jax.random.key(seed), 5)
    right_side = scatter_about(splits[0], (NX, NY, NZ), 4.0, 24.0, ((0, 16), (1, 8)), jnp.float32)
    alpha_coef = jnp.clip(jnp.exp(math.log(0.5) - 2.3025851 * jax.random.uniform(splits[1], (NX, NY, NZ), jnp.float32) ** block_levels(splits[1], (NX, NY, NZ), ((0, 16), (1, 8)), -0.2, 0.2)), 0.05, 0.5)
    face_coef = jnp.clip(jnp.exp(math.log(4.0) - 2.7725887 * jax.random.uniform(splits[2], (3, NX, NY, NZ), jnp.float32) ** block_levels(splits[2], (3, NX, NY, NZ), ((1, 16), (2, 8)), -0.2, 0.2)), 0.25, 4.0)
    owner_map = draw_owner_map(jax.random.fold_in(splits[4], 71), 0)
    return {"right_side": right_side, "alpha_coef": alpha_coef, "face_coef": face_coef, "owner_map": owner_map}


cheb_high = 2.0
cheb_low = 0.25


def shift_lower(field):
    return jnp.concatenate([jnp.zeros_like(field[..., :1]), field[..., :-1]], axis=-1)


def shift_upper(field):
    return jnp.concatenate([field[..., 1:], jnp.zeros_like(field[..., :1])], axis=-1)


def apply_operator(padded, alpha_inner, faces_padded):
    center = padded[1:-1, 1:-1]
    face_x = faces_padded[0, 1:-1, 1:-1]
    face_xu = faces_padded[0, 2:, 1:-1]
    face_y = faces_padded[1, 1:-1, 1:-1]
    face_yu = faces_padded[1, 1:-1, 2:]
    face_z = faces_padded[2, 1:-1, 1:-1]
    face_zu = shift_upper(face_z)
    result = alpha_inner * center
    result = result + face_x * (center - padded[:-2, 1:-1]) + face_xu * (center - padded[2:, 1:-1])
    result = result + face_y * (center - padded[1:-1, :-2]) + face_yu * (center - padded[1:-1, 2:])
    result = result + face_z * (center - shift_lower(center)) + face_zu * (center - shift_upper(center))
    return result


def diagonal_of(alpha_inner, faces_padded):
    face_x = faces_padded[0, 1:-1, 1:-1]
    face_xu = faces_padded[0, 2:, 1:-1]
    face_y = faces_padded[1, 1:-1, 1:-1]
    face_yu = faces_padded[1, 1:-1, 2:]
    face_z = faces_padded[2, 1:-1, 1:-1]
    return alpha_inner + face_x + face_xu + face_y + face_yu + face_z + shift_upper(face_z)


def pad_cells(field):
    return jnp.pad(field, ((1, 1), (1, 1), (0, 0)))


def average_cells(field):
    shaped = field.reshape(field.shape[0] // 2, 2, field.shape[1] // 2, 2, field.shape[2] // 2, 2)
    return jnp.sum(shaped, axis=(1, 3, 5)) * 0.125


def average_faces(faces):
    shaped = faces.reshape(3, faces.shape[1] // 2, 2, faces.shape[2] // 2, 2, faces.shape[3] // 2, 2)
    along_x = jnp.sum(shaped[0][:, 0], axis=(2, 4)) * 0.25
    along_y = jnp.sum(shaped[1][:, :, :, 0], axis=(1, 4)) * 0.25
    along_z = jnp.sum(shaped[2][..., 0], axis=(1, 3)) * 0.25
    return [along_x, along_y, along_z]


def owner_tiles(coarse, order):
    shaped = coarse.reshape(N_GX, HALF, N_GY, HALF, TZ, HALF)
    tiles = shaped.transpose(2, 0, 4, 3, 1, 5).reshape(N_GY, TILES, HALF, HALF * HALF)
    ordered = jnp.take_along_axis(tiles, order[:, :, None, None], axis=1)
    return ordered.transpose(1, 0, 2, 3).reshape(TILES, N_GY * HALF, HALF * HALF)


def reference(right_side, alpha_coef, face_coef, owner_map):
    theta_mid = (cheb_high + cheb_low) / 2.0
    delta_half = (cheb_high - cheb_low) / 2.0
    sigma_ratio = theta_mid / delta_half
    faces_padded = jnp.pad(face_coef, ((0, 0), (1, 1), (1, 1), (0, 0)))
    inverse = 1.0 / diagonal_of(alpha_coef, faces_padded)
    solution = inverse * right_side / theta_mid
    update = solution
    rho_prev = 1.0 / sigma_ratio
    for _ in range(ITERS - 1):
        residual = right_side - apply_operator(pad_cells(solution), alpha_coef, faces_padded)
        rho_next = 1.0 / (2.0 * sigma_ratio - rho_prev)
        update = rho_next * rho_prev * update + (2.0 * rho_next / delta_half) * inverse * residual
        solution = solution + update
        rho_prev = rho_next
    residual = right_side - apply_operator(pad_cells(solution), alpha_coef, faces_padded)
    order = jnp.argsort(owner_map, axis=1, stable=True).astype(jnp.int32)
    coarse_residual = owner_tiles(average_cells(residual), order)
    fields = [average_cells(alpha_coef)] + average_faces(face_coef)
    coarse_coef = jnp.stack([owner_tiles(field, order) for field in fields])
    return solution, coarse_residual, coarse_coef
```

```python
import functools

import jax
import jax.numpy as jnp
from jax import lax
from jax.experimental import pallas as pl
from jax.experimental.pallas import tpu as pltpu
from jax.sharding import PartitionSpec as P

ITERS = 4
CHEB_HIGH = 2.0
CHEB_LOW = 0.25

MESH = pl.DeviceIdType.MESH
LANES = 128
N_GX = 16
Y0 = 8


def chebyshev_steps():
    theta = (CHEB_HIGH + CHEB_LOW) / 2.0
    delta = (CHEB_HIGH - CHEB_LOW) / 2.0
    sigma = theta / delta
    rho = 1.0 / sigma
    steps = []
    for _ in range(ITERS - 1):
        rho_next = 1.0 / (2.0 * sigma - rho)
        steps.append((rho_next * rho, 2.0 * rho_next / delta))
        rho = rho_next
    return theta, steps


def kernel(
    n_gy,
    owner_ref,
    b_hbm,
    alpha_hbm,
    face_hbm,
    sol_hbm,
    cres_hbm,
    ccoef_hbm,
    B,
    AL,
    FX,
    FY,
    FZ,
    FZU,
    INV,
    DG,
    V,
    RES,
    YP,
    YR,
    FYP,
    FYR,
    SB,
    CB,
    T,
    RA,
    RB,
    RC,
    S2,
    box_of,
    load_sem,
    face_send,
    face_recv,
    halo_send,
    halo_recv,
    one_send,
    one_recv,
    one_local,
    two_send,
    two_recv,
    two_local,
    out_sem,
):
    nx, ny = 32, 32
    nl = 4
    gx = lax.axis_index("gx")
    gy = lax.axis_index("gy")
    bx, r = gx // 4, gx % 4
    theta, steps = chebyshev_steps()

    def load(src, dst, which, lt):
        return pltpu.make_async_copy(src, dst, load_sem.at[which, lt])

    loads = []
    for lt in range(nl):
        cols = pl.ds(lt * LANES, LANES)
        loads.append(
            [
                load(face_hbm.at[0, :, :, cols], FX.at[lt, pl.ds(0, nx)], 0, lt),
                load(face_hbm.at[1, :, :, cols], FY.at[lt, :, pl.ds(0, ny)], 1, lt),
                load(face_hbm.at[2, :, :, cols], FZ.at[lt], 2, lt),
                load(alpha_hbm.at[:, :, cols], AL.at[lt], 3, lt),
                load(b_hbm.at[:, :, cols], B.at[lt], 4, lt),
            ]
        )
    for which in range(5):
        for lt in range(nl):
            loads[lt][which].start()

    zero_plane = jnp.zeros((ny, LANES), jnp.float32)
    for lt in range(nl):
        FX[lt, nx] = zero_plane
        FYR[lt] = zero_plane
        for k in range(ITERS):
            V[k, lt, 0, Y0 : Y0 + ny] = zero_plane
            V[k, lt, nx + 1, Y0 : Y0 + ny] = zero_plane
            YR[k, 0, lt] = zero_plane
            YR[k, 1, lt] = zero_plane

    barrier = pltpu.get_barrier_semaphore()

    @pl.loop(1, N_GX)
    def _(d):
        pl.semaphore_signal(
            barrier, inc=1, device_id=(lax.rem(gx + d, N_GX), gy), device_id_type=MESH
        )

    has_up = gy < n_gy - 1
    has_down = gy > 0

    @pl.when(has_down)
    def _():
        pl.semaphore_signal(barrier, inc=1, device_id=(gx, gy - 1), device_id_type=MESH)

    @pl.when(has_up)
    def _():
        pl.semaphore_signal(barrier, inc=1, device_id=(gx, gy + 1), device_id_type=MESH)

    owners = [owner_ref[0, (4 * (b // 4)) * 16 + 4 * (b % 4)] for b in range(16)]
    for o in range(16):
        found = jnp.int32(0)
        for b in range(16):
            found = jnp.where(owners[b] == o, jnp.int32(b), found)
        box_of[o] = found

    sides = jnp.where(has_down, 1, 0) + jnp.where(has_up, 1, 0)
    pl.semaphore_wait(barrier, N_GX - 1 + sides)

    def remote(src, dst, send, recv, to_x, to_y):
        return pltpu.make_async_remote_copy(
            src_ref=src,
            dst_ref=dst,
            send_sem=send,
            recv_sem=recv,
            device_id=(to_x, to_y),
            device_id_type=MESH,
        )

    def guarded(pred, fn):
        @pl.when(pred)
        def _():
            fn()

    x_low, x_high = gx > 0, gx < N_GX - 1

    face_x = remote(
        FX.at[:, pl.ds(0, 1)], FX.at[:, pl.ds(nx, 1)], face_send.at[0], face_recv.at[0], gx - 1, gy
    )
    face_y = remote(FYP, FYR, face_send.at[1], face_recv.at[1], gx, gy - 1)
    for lt in range(nl):
        loads[lt][0].wait()
    guarded(x_low, face_x.start)
    fy_flat = FY.reshape(nl, nx * 40, LANES)
    for lt in range(nl):
        loads[lt][1].wait()
        FYP[lt] = fy_flat[lt, pl.ds(0, nx, stride=40), :]
    guarded(has_down, face_y.start)
    for which in range(2, 5):
        for lt in range(nl):
            loads[lt][which].wait()

    lane = lax.broadcasted_iota(jnp.int32, (8, LANES), 1)
    first_lane, last_lane = lane == 0, lane == LANES - 1
    blank = jnp.zeros((8, LANES), jnp.float32)

    def z_lower(c):
        turned = [pltpu.roll(ci, 1, axis=1) for ci in c]
        return [
            jnp.where(first_lane, turned[i - 1] if i else blank, turned[i]) for i in range(nl)
        ]

    def z_upper(c):
        turned = [pltpu.roll(ci, LANES - 1, axis=1) for ci in c]
        return [
            jnp.where(last_lane, turned[i + 1] if i < nl - 1 else blank, turned[i])
            for i in range(nl)
        ]

    v_flat = V.reshape(ITERS, nl, (nx + 2) * 48, LANES)

    def halo_copies(k):
        rows = pl.ds(Y0, ny)
        down_x = remote(
            V.at[k, :, pl.ds(1, 1), rows],
            V.at[k, :, pl.ds(nx + 1, 1), rows],
            halo_send.at[k, 0],
            halo_recv.at[k, 0],
            gx - 1,
            gy,
        )
        up_x = remote(
            V.at[k, :, pl.ds(nx, 1), rows],
            V.at[k, :, pl.ds(0, 1), rows],
            halo_send.at[k, 1],
            halo_recv.at[k, 1],
            gx + 1,
            gy,
        )
        down_y = remote(YP.at[k, 0], YR.at[k, 1], halo_send.at[k, 2], halo_recv.at[k, 2], gx, gy - 1)
        up_y = remote(YP.at[k, 1], YR.at[k, 0], halo_send.at[k, 3], halo_recv.at[k, 3], gx, gy + 1)
        return down_x, up_x, down_y, up_y

    halos = [halo_copies(k) for k in range(ITERS)]

    def send_y(k):
        for lt in range(nl):
            YP[k, 0, lt] = v_flat[k, lt, pl.ds(48 + Y0, nx, stride=48), :]
            YP[k, 1, lt] = v_flat[k, lt, pl.ds(48 + Y0 + ny - 1, nx, stride=48), :]
        guarded(has_down, halos[k][2].start)
        guarded(has_up, halos[k][3].start)

    def send_x(k):
        guarded(x_low, halos[k][0].start)
        guarded(x_high, halos[k][1].start)

    def wait_halo(k):
        down_x, up_x, down_y, up_y = halos[k]
        guarded(x_low, down_x.wait_send)
        guarded(x_high, down_x.wait_recv)
        guarded(x_high, up_x.wait_send)
        guarded(x_low, up_x.wait_recv)
        guarded(has_down, down_y.wait_send)
        guarded(has_up, down_y.wait_recv)
        guarded(has_up, up_y.wait_send)
        guarded(has_down, up_y.wait_recv)
        for lt in range(nl):
            v_flat[k, lt, pl.ds(48 + Y0 - 1, nx, stride=48), :] = YR[k, 0, lt]
            v_flat[k, lt, pl.ds(48 + Y0 + ny, nx, stride=48), :] = YR[k, 1, lt]

    def in_parts(body):
        def loop(lo, hi, tiles):
            def step(x, carry):
                body(x, tiles)
                return carry

            lax.fori_loop(lo, hi, step, 0)

        return (
            lambda: loop(0, nx, (0, 3)),
            lambda: (body(0, (1, 2)), body(nx - 1, (1, 2))),
            lambda: loop(1, nx - 1, (1, 2)),
        )

    def first(x, tiles):
        for yt in tiles:
            rows = pl.ds(8 * yt, 8)
            fz = [FZ[lt, x, rows, :] for lt in range(nl)]
            fzu = z_upper(fz)
            for lt in range(nl):
                d = AL[lt, x, rows, :] + FX[lt, x, rows, :] + FX[lt, x + 1, rows, :]
                d = d + FY[lt, x, rows, :] + FY[lt, x, pl.ds(8 * yt + 1, 8), :]
                d = d + fz[lt] + fzu[lt]
                inv = 1.0 / d
                FZU[lt, x, rows, :] = fzu[lt]
                DG[lt, x, rows, :] = d
                INV[lt, x, rows, :] = inv
                V[0, lt, x + 1, pl.ds(Y0 + 8 * yt, 8), :] = inv * B[lt, x, rows, :] * (1.0 / theta)

    def gathered(k, x, yt):
        rows = pl.ds(8 * yt, 8)
        y = Y0 + 8 * yt
        c = [V[k, lt, x + 1, pl.ds(y, 8), :] for lt in range(nl)]
        low, high = z_lower(c), z_upper(c)
        t = []
        for lt in range(nl):
            s = B[lt, x, rows, :] + FX[lt, x, rows, :] * V[k, lt, x, pl.ds(y, 8), :]
            s = s + FX[lt, x + 1, rows, :] * V[k, lt, x + 2, pl.ds(y, 8), :]
            s = s + FY[lt, x, rows, :] * V[k, lt, x + 1, pl.ds(y - 1, 8), :]
            s = s + FY[lt, x, pl.ds(8 * yt + 1, 8), :] * V[k, lt, x + 1, pl.ds(y + 1, 8), :]
            s = s + FZ[lt, x, rows, :] * low[lt] + FZU[lt, x, rows, :] * high[lt]
            t.append(s)
        return t, c

    def sweep(k, c1, c2):
        def body(x, tiles):
            for yt in tiles:
                t, c = gathered(k, x, yt)
                rows = pl.ds(8 * yt, 8)
                y = pl.ds(Y0 + 8 * yt, 8)
                for lt in range(nl):
                    new = (1.0 + c1 - c2) * c[lt] + c2 * (INV[lt, x, rows, :] * t[lt])
                    if k > 0:
                        new = new - c1 * V[k - 1, lt, x + 1, y, :]
                    V[k + 1, lt, x + 1, y, :] = new

        return body

    row_i = lax.broadcasted_iota(jnp.int32, (LANES, LANES), 0)
    col_i = lax.broadcasted_iota(jnp.int32, (LANES, LANES), 1)
    groups = [(lane // 16) // d % 2 == 1 for d in (4, 2, 1)]

    def restrict(f, pairs, weight, even_only):
        def gather(X, carry):
            for lt in range(nl):
                SB[lt, pl.ds(pl.multiple_of(X * 16, 16), 16), :] = pairs(lt, X)
            return carry

        lax.fori_loop(0, 16, gather, 0)
        for half in range(2):
            total = None
            for side in range(2):
                hit = row_i // 2 + 64 * side == col_i
                if even_only:
                    hit = hit & (row_i % 2 == 0)
                pick = jnp.where(hit, weight, 0.0).astype(jnp.float32)
                part = jnp.dot(
                    SB[2 * half + side],
                    pick,
                    precision=lax.Precision.HIGHEST,
                    preferred_element_type=jnp.float32,
                )
                total = part if total is None else total + part
            CB[half] = total.reshape(16, 16, LANES)

        def turn(i, carry):
            half, yt, xt = i // 4, i // 2 % 2, i % 2
            rows = pl.ds(pl.multiple_of(yt * 8, 8), 8)
            a = [CB[half, xt * 8 + j, rows, :] for j in range(8)]
            for d, odd in zip((4, 2, 1), groups):
                b = list(a)
                for j in range(8):
                    if j & d == 0:
                        lo, hi = a[j], a[j + d]
                        b[j] = jnp.where(odd, pltpu.roll(hi, 16 * d, axis=1), lo)
                        b[j + d] = jnp.where(odd, hi, pltpu.roll(lo, LANES - 16 * d, axis=1))
                a = b
            for j in range(8):
                T[f, yt * 2 + xt, half * 2 + j // 4, j % 4] = a[j]
            return carry

        lax.fori_loop(0, 8, turn, 0)

    def strided(ref, lt, x, start):
        return ref[lt, x, pl.ds(start, 16, stride=2), :]

    def four(ref):
        return lambda lt, X: (
            strided(ref, lt, 2 * X, 0)
            + strided(ref, lt, 2 * X, 1)
            + strided(ref, lt, 2 * X + 1, 0)
            + strided(ref, lt, 2 * X + 1, 1)
        )

    spread = (RA, RB, RC)

    def stage_one(f):
        copies = []
        for j in range(1, 4):
            q = lax.rem(bx + j, 4)
            copies.append(
                remote(
                    T.at[f, q],
                    spread[f // 2].at[f % 2, pl.ds(bx * 4, 4)],
                    one_send.at[f, j],
                    one_recv.at[f, j],
                    q * 4 + r,
                    gy,
                )
            )
        own = pltpu.make_async_copy(T.at[f, bx], spread[f // 2].at[f % 2, pl.ds(bx * 4, 4)], one_local.at[f])
        return copies, own

    first_stage = [stage_one(f) for f in range(5)]

    def start_one(f):
        copies, own = first_stage[f]
        for c in copies:
            c.start()
        own.start()

    def wait_one(f):
        copies, own = first_stage[f]
        for c in copies:
            c.wait()
        own.wait()

    yt, xt = bx // 2, bx % 2
    out_rows = pl.ds(pl.multiple_of(r * 4, 4), 4)
    out_y = pl.ds(pl.multiple_of(yt * 8, 8), 8)
    out_cols = pl.ds(pl.multiple_of(xt * LANES, LANES), LANES)
    group_fields = ((0, 2), (2, 4), (4, 5))

    def landing(g):
        lo, hi = group_fields[g]
        if g == 2:
            return cres_hbm.at[:, out_rows, out_y, out_cols]
        return ccoef_hbm.at[pl.ds(lo, hi - lo), out_rows, out_y, out_cols]

    def two_copy(g, d):
        lo, hi = group_fields[g]
        o = lax.rem(gx + d, N_GX)
        return remote(
            S2.at[o, pl.ds(lo, hi - lo)], landing(g), two_send.at[g, d], two_recv.at[g, d], o, gy
        )

    def two_own(g):
        lo, hi = group_fields[g]
        return pltpu.make_async_copy(S2.at[gx, pl.ds(lo, hi - lo)], landing(g), two_local.at[g])

    def start_two(g):
        lo, hi = group_fields[g]

        def pack(o, carry):
            box = box_of[o]
            for f in range(lo, hi):
                S2[o, f] = spread[g][f - lo, box]
            return carry

        lax.fori_loop(0, N_GX, pack, 0)

        @pl.loop(1, N_GX)
        def _(d):
            two_copy(g, d).start()

        two_own(g).start()

    def wait_two(g):
        @pl.loop(1, N_GX)
        def _(d):
            two_copy(g, d).wait()

        two_own(g).wait()

    guarded(x_high, face_x.wait_recv)
    guarded(x_low, face_x.wait_send)
    guarded(has_up, face_y.wait_recv)
    guarded(has_down, face_y.wait_send)
    for lt in range(nl):
        fy_flat[lt, pl.ds(ny, nx, stride=40), :] = FYR[lt]

    def all_parts(k, body):
        y_part, x_part, inner = in_parts(body)
        y_part()
        send_y(k)
        x_part()
        send_x(k)
        inner()

    all_parts(0, first)
    restrict(0, four(AL), 0.125, False)
    start_one(0)
    restrict(
        1, lambda lt, X: strided(FX, lt, 2 * X, 0) + strided(FX, lt, 2 * X, 1), 0.25, False
    )
    start_one(1)
    wait_halo(0)
    all_parts(1, sweep(0, *steps[0]))
    restrict(
        2, lambda lt, X: strided(FY, lt, 2 * X, 0) + strided(FY, lt, 2 * X + 1, 0), 0.25, False
    )
    start_one(2)
    restrict(3, four(FZ), 0.25, True)
    start_one(3)
    wait_halo(1)
    all_parts(2, sweep(1, *steps[1]))
    wait_one(0)
    wait_one(1)
    start_two(0)
    wait_halo(2)
    all_parts(3, sweep(2, *steps[2]))
    outs = [
        pltpu.make_async_copy(
            V.at[3, lt, pl.ds(1, nx), pl.ds(Y0, ny)],
            sol_hbm.at[:, :, pl.ds(lt * LANES, LANES)],
            out_sem.at[lt],
        )
        for lt in range(nl)
    ]
    for o in outs:
        o.start()
    wait_one(2)
    wait_one(3)
    start_two(1)
    wait_halo(3)

    def last(X, carry):
        for yt_ in range(4):
            rows = pl.ds(8 * yt_, 8)
            acc = None
            for a in range(2):
                x = 2 * X + a
                t, c = gathered(3, x, yt_)
                res = [t[lt] - DG[lt, x, rows, :] * c[lt] for lt in range(nl)]
                acc = res if acc is None else [p + q for p, q in zip(acc, res)]
            for lt in range(nl):
                RES[lt, X, rows, :] = acc[lt]
        return carry

    lax.fori_loop(0, 16, last, 0)
    restrict(4, lambda lt, X: strided(RES, lt, X, 0) + strided(RES, lt, X, 1), 0.125, False)
    start_one(4)
    wait_one(4)
    start_two(2)
    for o in outs:
        o.wait()
    for g in range(3):
        wait_two(g)


def local(n_gy, right_side, alpha_coef, face_coef, owner_map):
    f32 = jnp.float32
    vmem = pltpu.VMEM
    dma = pltpu.SemaphoreType.DMA
    hbm = pl.BlockSpec(memory_space=pl.ANY)
    cells = vmem((4, 32, 32, LANES), f32)
    sol, cres, ccoef = pl.pallas_call(
        functools.partial(kernel, n_gy),
        out_shape=(
            jax.ShapeDtypeStruct((32, 32, 512), f32),
            jax.ShapeDtypeStruct((1, 16, 16, 256), f32),
            jax.ShapeDtypeStruct((4, 16, 16, 256), f32),
        ),
        in_specs=[pl.BlockSpec(memory_space=pltpu.SMEM), hbm, hbm, hbm],
        out_specs=(hbm, hbm, hbm),
        scratch_shapes=[
            cells,
            cells,
            vmem((4, 33, 32, LANES), f32),
            vmem((4, 32, 40, LANES), f32),
            cells,
            cells,
            cells,
            cells,
            vmem((ITERS, 4, 34, 48, LANES), f32),
            vmem((4, 16, 32, LANES), f32),
            vmem((ITERS, 2, 4, 32, LANES), f32),
            vmem((ITERS, 2, 4, 32, LANES), f32),
            vmem((4, 32, LANES), f32),
            vmem((4, 32, LANES), f32),
            vmem((4, 256, LANES), f32),
            vmem((2, 16, 16, LANES), f32),
            vmem((5, 4, 4, 4, 8, LANES), f32),
            vmem((2, 16, 4, 8, LANES), f32),
            vmem((2, 16, 4, 8, LANES), f32),
            vmem((1, 16, 4, 8, LANES), f32),
            vmem((16, 5, 4, 8, LANES), f32),
            pltpu.SMEM((16,), jnp.int32),
            dma((5, 4)),
            dma((2,)),
            dma((2,)),
            dma((ITERS, 4)),
            dma((ITERS, 4)),
            dma((5, 4)),
            dma((5, 4)),
            dma((5,)),
            dma((3, 16)),
            dma((3, 16)),
            dma((3,)),
            dma((4,)),
        ],
        compiler_params=pltpu.CompilerParams(
            collective_id=0, has_side_effects=True, vmem_limit_bytes=56 << 20
        ),
        name="smooth_and_restrict",
    )(owner_map, right_side, alpha_coef, face_coef)
    return sol, cres[0], ccoef


def solution(mesh):
    return jax.shard_map(
        functools.partial(local, mesh.shape["gy"]),
        mesh=mesh,
        in_specs=(
            P("gx", "gy", None),
            P("gx", "gy", None),
            P(None, "gx", "gy", None),
            P("gy", None),
        ),
        out_specs=(P("gx", "gy", None), P("gx", "gy", None), P(None, "gx", "gy", None)),
        check_vma=False,
    )
```

```python
import functools

import jax
import jax.numpy as jnp
from jax import lax
from jax.experimental import pallas as pl
from jax.experimental.pallas import tpu as pltpu
from jax.sharding import PartitionSpec as P

ITERS = 4
CHEB_HIGH = 2.0
CHEB_LOW = 0.25

MESH = pl.DeviceIdType.MESH
LANES = 128
N_GX = 16
Y0 = 8


def chebyshev_steps():
    theta = (CHEB_HIGH + CHEB_LOW) / 2.0
    delta = (CHEB_HIGH - CHEB_LOW) / 2.0
    sigma = theta / delta
    rho = 1.0 / sigma
    steps = []
    for _ in range(ITERS - 1):
        rho_next = 1.0 / (2.0 * sigma - rho)
        steps.append((rho_next * rho, 2.0 * rho_next / delta))
        rho = rho_next
    return theta, steps


def kernel(
    n_gy,
    owner_ref,
    b_hbm,
    alpha_hbm,
    face_hbm,
    sol_ref,
    cres_ref,
    ccoef_ref,
    B,
    AL,
    FX,
    FY,
    FZ,
    FZU,
    INV,
    DG,
    V,
    RES,
    YP,
    YR,
    FYP,
    FYR,
    SB,
    CB,
    T,
    RA,
    RB,
    RC,
    RD,
    RE,
    S2,
    box_of,
    load_sem,
    face_send,
    face_recv,
    halo_send,
    halo_recv,
    one_send,
    one_recv,
    one_local,
    two_send,
    two_recv,
    two_local,
):
    nx, ny = 32, 32
    nl = 4
    gx = lax.axis_index("gx")
    gy = lax.axis_index("gy")
    bx, r = gx // 4, gx % 4
    theta, steps = chebyshev_steps()

    def load(src, dst, which, lt):
        return pltpu.make_async_copy(src, dst, load_sem.at[which, lt])

    loads = []
    for lt in range(nl):
        cols = pl.ds(lt * LANES, LANES)
        loads.append(
            [
                load(face_hbm.at[0, :, :, cols], FX.at[lt, pl.ds(0, nx)], 0, lt),
                load(face_hbm.at[1, :, :, cols], FY.at[lt, :, pl.ds(0, ny)], 1, lt),
                load(face_hbm.at[2, :, :, cols], FZ.at[lt], 2, lt),
                load(alpha_hbm.at[:, :, cols], AL.at[lt], 3, lt),
                load(b_hbm.at[:, :, cols], B.at[lt], 4, lt),
            ]
        )
    for which in range(5):
        for lt in range(nl):
            loads[lt][which].start()

    zero_plane = jnp.zeros((ny, LANES), jnp.float32)
    for lt in range(nl):
        FX[lt, nx] = zero_plane
        FYR[lt] = zero_plane
        for k in range(ITERS):
            V[k, lt, 0, Y0 : Y0 + ny] = zero_plane
            V[k, lt, nx + 1, Y0 : Y0 + ny] = zero_plane
            YR[k, 0, lt] = zero_plane
            YR[k, 1, lt] = zero_plane

    barrier = pltpu.get_barrier_semaphore()

    @pl.loop(1, N_GX)
    def _(d):
        pl.semaphore_signal(
            barrier, inc=1, device_id=(lax.rem(gx + d, N_GX), gy), device_id_type=MESH
        )

    has_up = gy < n_gy - 1
    has_down = gy > 0

    @pl.when(has_down)
    def _():
        pl.semaphore_signal(barrier, inc=1, device_id=(gx, gy - 1), device_id_type=MESH)

    @pl.when(has_up)
    def _():
        pl.semaphore_signal(barrier, inc=1, device_id=(gx, gy + 1), device_id_type=MESH)

    owners = [owner_ref[0, (4 * (b // 4)) * 16 + 4 * (b % 4)] for b in range(16)]
    for o in range(16):
        found = jnp.int32(0)
        for b in range(16):
            found = jnp.where(owners[b] == o, jnp.int32(b), found)
        box_of[o] = found

    sides = jnp.where(has_down, 1, 0) + jnp.where(has_up, 1, 0)
    pl.semaphore_wait(barrier, N_GX - 1 + sides)

    def remote(src, dst, send, recv, to_x, to_y):
        return pltpu.make_async_remote_copy(
            src_ref=src,
            dst_ref=dst,
            send_sem=send,
            recv_sem=recv,
            device_id=(to_x, to_y),
            device_id_type=MESH,
        )

    def guarded(pred, fn):
        @pl.when(pred)
        def _():
            fn()

    x_low, x_high = gx > 0, gx < N_GX - 1

    face_x = remote(
        FX.at[:, pl.ds(0, 1)], FX.at[:, pl.ds(nx, 1)], face_send.at[0], face_recv.at[0], gx - 1, gy
    )
    face_y = remote(FYP, FYR, face_send.at[1], face_recv.at[1], gx, gy - 1)
    fy_flat = FY.reshape(nl, nx * 40, LANES)

    def wait_load(which):
        for lt in range(nl):
            loads[lt][which].wait()

    wait_load(0)
    guarded(x_low, face_x.start)
    wait_load(1)
    for lt in range(nl):
        FYP[lt] = fy_flat[lt, pl.ds(0, nx, stride=40), :]
    guarded(has_down, face_y.start)

    lane = lax.broadcasted_iota(jnp.int32, (8, LANES), 1)
    first_lane, last_lane = lane == 0, lane == LANES - 1
    blank = jnp.zeros((8, LANES), jnp.float32)

    def z_lower(c):
        turned = [pltpu.roll(ci, 1, axis=1) for ci in c]
        return [
            jnp.where(first_lane, turned[i - 1] if i else blank, turned[i]) for i in range(nl)
        ]

    def z_upper(c):
        turned = [pltpu.roll(ci, LANES - 1, axis=1) for ci in c]
        return [
            jnp.where(last_lane, turned[i + 1] if i < nl - 1 else blank, turned[i])
            for i in range(nl)
        ]

    v_flat = V.reshape(ITERS, nl, (nx + 2) * 48, LANES)

    def halo_copies(k):
        rows = pl.ds(Y0, ny)
        down_x = remote(
            V.at[k, :, pl.ds(1, 1), rows],
            V.at[k, :, pl.ds(nx + 1, 1), rows],
            halo_send.at[k, 0],
            halo_recv.at[k, 0],
            gx - 1,
            gy,
        )
        up_x = remote(
            V.at[k, :, pl.ds(nx, 1), rows],
            V.at[k, :, pl.ds(0, 1), rows],
            halo_send.at[k, 1],
            halo_recv.at[k, 1],
            gx + 1,
            gy,
        )
        down_y = remote(YP.at[k, 0], YR.at[k, 1], halo_send.at[k, 2], halo_recv.at[k, 2], gx, gy - 1)
        up_y = remote(YP.at[k, 1], YR.at[k, 0], halo_send.at[k, 3], halo_recv.at[k, 3], gx, gy + 1)
        return down_x, up_x, down_y, up_y

    halos = [halo_copies(k) for k in range(ITERS)]

    def send_y(k):
        guarded(has_down, halos[k][2].start)
        guarded(has_up, halos[k][3].start)

    def send_x(k):
        guarded(x_low, halos[k][0].start)
        guarded(x_high, halos[k][1].start)

    def wait_halo(k):
        down_x, up_x, down_y, up_y = halos[k]
        guarded(x_low, down_x.wait_send)
        guarded(x_high, down_x.wait_recv)
        guarded(x_high, up_x.wait_send)
        guarded(x_low, up_x.wait_recv)
        guarded(has_down, down_y.wait_send)
        guarded(has_up, down_y.wait_recv)
        guarded(has_up, up_y.wait_send)
        guarded(has_down, up_y.wait_recv)
        for lt in range(nl):
            v_flat[k, lt, pl.ds(48 + Y0 - 1, nx, stride=48), :] = YR[k, 0, lt]
            v_flat[k, lt, pl.ds(48 + Y0 + ny, nx, stride=48), :] = YR[k, 1, lt]

    def planes(body, lo, hi, tiles, unroll):
        def step(x, carry):
            body(x, tiles)
            return carry

        lax.fori_loop(lo, hi, step, 0, unroll=unroll)

    def first(x, tiles):
        for yt in tiles:
            rows = pl.ds(8 * yt, 8)
            fz = [FZ[lt, x, rows, :] for lt in range(nl)]
            fzu = z_upper(fz)
            for lt in range(nl):
                d = AL[lt, x, rows, :] + FX[lt, x, rows, :] + FX[lt, x + 1, rows, :]
                d = d + FY[lt, x, rows, :] + FY[lt, x, pl.ds(8 * yt + 1, 8), :]
                d = d + fz[lt] + fzu[lt]
                inv = 1.0 / d
                FZU[lt, x, rows, :] = fzu[lt]
                DG[lt, x, rows, :] = d
                INV[lt, x, rows, :] = inv
                V[0, lt, x + 1, pl.ds(Y0 + 8 * yt, 8), :] = inv * B[lt, x, rows, :] * (1.0 / theta)

    def gathered(k, x, yt):
        rows = pl.ds(8 * yt, 8)
        y = Y0 + 8 * yt
        c = [V[k, lt, x + 1, pl.ds(y, 8), :] for lt in range(nl)]
        low, high = z_lower(c), z_upper(c)
        t = []
        for lt in range(nl):
            s = B[lt, x, rows, :] + FX[lt, x, rows, :] * V[k, lt, x, pl.ds(y, 8), :]
            s = s + FX[lt, x + 1, rows, :] * V[k, lt, x + 2, pl.ds(y, 8), :]
            s = s + FY[lt, x, rows, :] * V[k, lt, x + 1, pl.ds(y - 1, 8), :]
            s = s + FY[lt, x, pl.ds(8 * yt + 1, 8), :] * V[k, lt, x + 1, pl.ds(y + 1, 8), :]
            s = s + FZ[lt, x, rows, :] * low[lt] + FZU[lt, x, rows, :] * high[lt]
            t.append(s)
        return t, c

    def sweep(k, c1, c2):
        def body(x, tiles):
            for yt in tiles:
                t, c = gathered(k, x, yt)
                rows = pl.ds(8 * yt, 8)
                y = pl.ds(Y0 + 8 * yt, 8)
                for lt in range(nl):
                    new = (1.0 + c1 - c2) * c[lt] + c2 * (INV[lt, x, rows, :] * t[lt])
                    if k > 0:
                        new = new - c1 * V[k - 1, lt, x + 1, y, :]
                    V[k + 1, lt, x + 1, y, :] = new
                    if k == ITERS - 2:
                        sol_ref[x, rows, lt * LANES : (lt + 1) * LANES] = new

        return body

    flat = {n: r.reshape(nl, nx * ny, LANES) for n, r in (("b", B), ("z", FZ), ("zu", FZU), ("inv", INV))}
    fx_flat = FX.reshape(nl, (nx + 1) * ny, LANES)

    def edge_rows(k, c1, c2):
        for side, y in ((0, 0), (1, ny - 1)):
            for j in range(nx // 8):

                def v_row(kk, lt, dx, dy):
                    return v_flat[
                        kk, lt, pl.ds((1 + 8 * j + dx) * 48 + Y0 + y + dy, 8, stride=48), :
                    ]

                def row(ref, lt, dx=0):
                    return ref[lt, pl.ds((8 * j + dx) * ny + y, 8, stride=ny), :]

                c = [v_row(k, lt, 0, 0) for lt in range(nl)]
                low, high = z_lower(c), z_upper(c)
                for lt in range(nl):
                    t = row(flat["b"], lt) + row(fx_flat, lt) * v_row(k, lt, -1, 0)
                    t = t + row(fx_flat, lt, 1) * v_row(k, lt, 1, 0)
                    at = 8 * j * 40 + y
                    t = t + fy_flat[lt, pl.ds(at, 8, stride=40), :] * v_row(k, lt, 0, -1)
                    t = t + fy_flat[lt, pl.ds(at + 1, 8, stride=40), :] * v_row(k, lt, 0, 1)
                    t = t + row(flat["z"], lt) * low[lt] + row(flat["zu"], lt) * high[lt]
                    new = (1.0 + c1 - c2) * c[lt] + c2 * (row(flat["inv"], lt) * t)
                    if k > 0:
                        new = new - c1 * v_row(k - 1, lt, 0, 0)
                    YP[k + 1, side, lt, 8 * j : 8 * j + 8] = new

    row_i = lax.broadcasted_iota(jnp.int32, (LANES, LANES), 0)
    col_i = lax.broadcasted_iota(jnp.int32, (LANES, LANES), 1)
    groups = [(lane // 16) // d % 2 == 1 for d in (4, 2, 1)]

    def restrict(f, pairs, weight, even_only, first_x=0, last_x=16):
        def gather(X, carry):
            for lt in range(nl):
                SB[lt, pl.ds(pl.multiple_of(X * 16, 16), 16), :] = pairs(lt, X)
            return carry

        lax.fori_loop(first_x, last_x, gather, 0, unroll=4)
        for half in range(2):
            total = None
            for side in range(2):
                hit = row_i // 2 + 64 * side == col_i
                if even_only:
                    hit = hit & (row_i % 2 == 0)
                pick = jnp.where(hit, weight, 0.0).astype(jnp.float32).astype(jnp.bfloat16)
                rest = SB[2 * half + side, first_x * 16 : last_x * 16]
                for _ in range(3):
                    piece = rest.astype(jnp.bfloat16)
                    rest = rest - piece.astype(jnp.float32)
                    part = jnp.dot(piece, pick, preferred_element_type=jnp.float32)
                    total = part if total is None else total + part
            CB[half, first_x:last_x] = total.reshape(last_x - first_x, 16, LANES)

        for half in range(2):
            for yt in range(2):
                for xt in range(first_x // 8, last_x // 8):
                    a = [CB[half, xt * 8 + j, 8 * yt : 8 * yt + 8, :] for j in range(8)]
                    for d, odd in zip((4, 2, 1), groups):
                        b = list(a)
                        for j in range(8):
                            if j & d == 0:
                                lo, hi = a[j], a[j + d]
                                b[j] = jnp.where(odd, pltpu.roll(hi, 16 * d, axis=1), lo)
                                b[j + d] = jnp.where(
                                    odd, hi, pltpu.roll(lo, LANES - 16 * d, axis=1)
                                )
                        a = b
                    for j in range(8):
                        T[f, yt * 2 + xt, half * 2 + j // 4, j % 4] = a[j]

    def strided(ref, lt, x, start):
        return ref[lt, x, pl.ds(start, 16, stride=2), :]

    def four(ref):
        return lambda lt, X: (
            strided(ref, lt, 2 * X, 0)
            + strided(ref, lt, 2 * X, 1)
            + strided(ref, lt, 2 * X + 1, 0)
            + strided(ref, lt, 2 * X + 1, 1)
        )

    spread = (RA, RB, RC, RD, RE)

    def stage_one(f):
        copies = []
        for j in range(1, 4):
            q = lax.rem(bx + j, 4)
            copies.append(
                remote(
                    T.at[f, q],
                    spread[f].at[pl.ds(bx * 4, 4)],
                    one_send.at[f, j],
                    one_recv.at[f, j],
                    q * 4 + r,
                    gy,
                )
            )
        own = pltpu.make_async_copy(T.at[f, bx], spread[f].at[pl.ds(bx * 4, 4)], one_local.at[f])
        return copies, own

    first_stage = [stage_one(f) for f in range(4)]

    def start_one(f):
        copies, own = first_stage[f]
        for c in copies:
            c.start()
        own.start()

    def wait_one(f):
        copies, own = first_stage[f]
        for c in copies:
            c.wait()
        own.wait()

    mine = RE.at[pl.ds(bx * 4, 4)]

    def residual_quarter(q, source):
        return remote(
            T.at[4, q], mine, one_send.at[4, q], one_recv.at[4, source], q * 4 + r, gy
        )

    own_quarter = pltpu.make_async_copy(T.at[4, bx], mine, one_local.at[4])

    def start_residual(q):
        guarded(bx != q, residual_quarter(q, bx).start)
        guarded(bx == q, own_quarter.start)

    def wait_residual():
        for q in range(4):
            guarded(bx != q, residual_quarter(q, bx).wait_send)
        for source in range(4):
            guarded(bx != source, residual_quarter(0, source).wait_recv)
        own_quarter.wait()

    yt, xt = bx // 2, bx % 2
    out_rows = pl.ds(pl.multiple_of(r * 4, 4), 4)
    out_y = pl.ds(pl.multiple_of(yt * 8, 8), 8)
    out_cols = pl.ds(pl.multiple_of(xt * LANES, LANES), LANES)

    def landing(f):
        if f == 4:
            return cres_ref.at[out_rows, out_y, out_cols]
        return ccoef_ref.at[f, out_rows, out_y, out_cols]

    def two_copy(f, d):
        o = lax.rem(gx + d, N_GX)
        return remote(S2.at[f, o], landing(f), two_send.at[f, d], two_recv.at[f, d], o, gy)

    def two_own(f):
        return pltpu.make_async_copy(S2.at[f, gx], landing(f), two_local.at[f])

    def start_two(f):
        def pack(o, carry):
            S2[f, o] = spread[f][box_of[o]]
            return carry

        lax.fori_loop(0, N_GX, pack, 0, unroll=4)

        @pl.loop(1, N_GX)
        def _(d):
            two_copy(f, d).start()

        two_own(f).start()

    def wait_two(f):
        @pl.loop(1, N_GX)
        def _(d):
            two_copy(f, d).wait()

        two_own(f).wait()

    def advance(k):
        body = sweep(k, *steps[k])
        body(0, (0, 1, 2, 3))
        body(nx - 1, (0, 1, 2, 3))
        send_x(k + 1)
        edge_rows(k, *steps[k])
        send_y(k + 1)
        planes(body, 1, nx - 1, (0, 1, 2, 3), 5)

    def restrict_y():
        def pairs(lt, X):
            return strided(FY, lt, 2 * X, 0) + strided(FY, lt, 2 * X + 1, 0)

        restrict(2, pairs, 0.25, False)

    def restrict_x():
        def pairs(lt, X):
            return strided(FX, lt, 2 * X, 0) + strided(FX, lt, 2 * X, 1)

        restrict(1, pairs, 0.25, False)

    restrict_y()
    start_one(2)
    for which in (2, 3, 4):
        wait_load(which)
    planes(first, 0, nx - 1, (0, 1, 2), 2)
    guarded(x_high, face_x.wait_recv)
    guarded(x_low, face_x.wait_send)
    guarded(has_up, face_y.wait_recv)
    guarded(has_down, face_y.wait_send)
    for lt in range(nl):
        fy_flat[lt, pl.ds(ny, nx, stride=40), :] = FYR[lt]
    first(nx - 1, (0, 1, 2))
    planes(first, 0, nx, (3,), 4)
    send_x(0)
    for lt in range(nl):
        YP[0, 0, lt] = v_flat[0, lt, pl.ds(48 + Y0, nx, stride=48), :]
        YP[0, 1, lt] = v_flat[0, lt, pl.ds(48 + Y0 + ny - 1, nx, stride=48), :]
    send_y(0)
    restrict(3, four(FZ), 0.25, True)
    start_one(3)
    restrict(0, four(AL), 0.125, False)
    start_one(0)
    wait_halo(0)
    advance(0)
    restrict_x()
    start_one(1)
    wait_one(2)
    start_two(2)
    wait_halo(1)
    advance(1)
    wait_one(3)
    start_two(3)
    wait_halo(2)
    advance(2)
    wait_one(0)
    start_two(0)

    def last(X, tiles):
        for yt_ in tiles:
            rows = pl.ds(8 * yt_, 8)
            acc = None
            for a in range(2):
                x = 2 * X + a
                t, c = gathered(3, x, yt_)
                res = [t[lt] - DG[lt, x, rows, :] * c[lt] for lt in range(nl)]
                acc = res if acc is None else [p + q for p, q in zip(acc, res)]
            for lt in range(nl):
                RES[lt, X, rows, :] = acc[lt]

    def restrict_residual(lo, hi):
        def pairs(lt, X):
            return strided(RES, lt, X, 0) + strided(RES, lt, X, 1)

        restrict(4, pairs, 0.125, False, lo, hi)

    planes(last, 1, 15, (1, 2), 2)
    wait_halo(3)
    last(0, (0, 1, 2, 3))
    planes(last, 1, 8, (0, 3), 7)
    restrict_residual(0, 8)
    start_residual(0)
    start_residual(2)
    planes(last, 8, 15, (0, 3), 7)
    last(15, (0, 1, 2, 3))
    restrict_residual(8, 16)
    start_residual(1)
    start_residual(3)
    wait_one(1)
    start_two(1)
    wait_residual()
    start_two(4)
    for f in range(5):
        wait_two(f)


def local(n_gy, right_side, alpha_coef, face_coef, owner_map):
    f32 = jnp.float32
    vmem = pltpu.VMEM
    dma = pltpu.SemaphoreType.DMA
    hbm = pl.BlockSpec(memory_space=pl.ANY)
    cells = vmem((4, 32, 32, LANES), f32)
    on_chip = pl.BlockSpec(memory_space=pltpu.VMEM)
    sol, cres, ccoef = pl.pallas_call(
        functools.partial(kernel, n_gy),
        out_shape=(
            vmem((32, 32, 512), f32),
            vmem((16, 16, 256), f32),
            vmem((4, 16, 16, 256), f32),
        ),
        in_specs=[pl.BlockSpec(memory_space=pltpu.SMEM), hbm, hbm, hbm],
        out_specs=(on_chip, on_chip, on_chip),
        scratch_shapes=[
            cells,
            cells,
            vmem((4, 33, 32, LANES), f32),
            vmem((4, 32, 40, LANES), f32),
            cells,
            cells,
            cells,
            cells,
            vmem((ITERS, 4, 34, 48, LANES), f32),
            vmem((4, 16, 32, LANES), f32),
            vmem((ITERS, 2, 4, 32, LANES), f32),
            vmem((ITERS, 2, 4, 32, LANES), f32),
            vmem((4, 32, LANES), f32),
            vmem((4, 32, LANES), f32),
            vmem((4, 256, LANES), f32),
            vmem((2, 16, 16, LANES), f32),
            vmem((5, 4, 4, 4, 8, LANES), f32),
            *[vmem((16, 4, 8, LANES), f32)] * 5,
            vmem((5, 16, 4, 8, LANES), f32),
            pltpu.SMEM((16,), jnp.int32),
            dma((5, 4)),
            dma((2,)),
            dma((2,)),
            dma((ITERS, 4)),
            dma((ITERS, 4)),
            dma((5, 4)),
            dma((5, 4)),
            dma((5,)),
            dma((5, 16)),
            dma((5, 16)),
            dma((5,)),
        ],
        compiler_params=pltpu.CompilerParams(
            collective_id=0, has_side_effects=True, vmem_limit_bytes=60 << 20
        ),
        name="smooth_and_restrict",
    )(owner_map, right_side, alpha_coef, face_coef)
    return sol, cres, ccoef


def solution(mesh):
    return jax.shard_map(
        functools.partial(local, mesh.shape["gy"]),
        mesh=mesh,
        in_specs=(
            P("gx", "gy", None),
            P("gx", "gy", None),
            P(None, "gx", "gy", None),
            P("gy", None),
        ),
        out_specs=(P("gx", "gy", None), P("gx", "gy", None), P(None, "gx", "gy", None)),
        check_vma=False,
    )
```

```python
import functools

import jax
import jax.numpy as jnp
from jax import lax
from jax.experimental import pallas as pl
from jax.experimental.pallas import tpu as pltpu
from jax.sharding import PartitionSpec as P

ITERS = 4
CHEB_HIGH = 2.0
CHEB_LOW = 0.25

MESH = pl.DeviceIdType.MESH
LANES = 128
N_GX = 16
Y0 = 8


def chebyshev_steps():
    theta = (CHEB_HIGH + CHEB_LOW) / 2.0
    delta = (CHEB_HIGH - CHEB_LOW) / 2.0
    sigma = theta / delta
    rho = 1.0 / sigma
    steps = []
    for _ in range(ITERS - 1):
        rho_next = 1.0 / (2.0 * sigma - rho)
        steps.append((rho_next * rho, 2.0 * rho_next / delta))
        rho = rho_next
    return theta, steps


def kernel(
    n_gy,
    owner_ref,
    b_hbm,
    alpha_hbm,
    face_hbm,
    sol_ref,
    cres_ref,
    ccoef_ref,
    B,
    AL,
    FX,
    FY,
    FZ,
    FZU,
    INV,
    DG,
    V,
    RES,
    YX,
    YR,
    EC,
    FYP,
    FYR,
    FXR,
    SB,
    CB,
    T,
    RA,
    RB,
    RC,
    RD,
    RE,
    S2,
    box_of,
    load_sem,
    face_send,
    face_recv,
    halo_send,
    halo_recv,
    one_send,
    one_recv,
    one_local,
    two_send,
    two_recv,
    two_local,
):
    nx, ny = 32, 32
    nl = 4
    gx = lax.axis_index("gx")
    gy = lax.axis_index("gy")
    bx, r = gx // 4, gx % 4
    theta, steps = chebyshev_steps()

    def load(src, dst, which, lt):
        return pltpu.make_async_copy(src, dst, load_sem.at[which, lt])

    loads = []
    for lt in range(nl):
        cols = pl.ds(lt * LANES, LANES)
        loads.append(
            [
                load(face_hbm.at[0, :, :, cols], FX.at[lt, pl.ds(0, nx)], 0, lt),
                load(face_hbm.at[1, :, :, cols], FY.at[lt, :, pl.ds(0, ny)], 1, lt),
                load(face_hbm.at[2, :, :, cols], FZ.at[lt], 2, lt),
                load(alpha_hbm.at[:, :, cols], AL.at[lt], 3, lt),
                load(b_hbm.at[:, :, cols], B.at[lt], 4, lt),
            ]
        )
    for which in range(5):
        for lt in range(nl):
            loads[lt][which].start()

    zero_plane = jnp.zeros((ny, LANES), jnp.float32)
    for lt in range(nl):
        FX[lt, nx] = zero_plane
        FXR[lt, 0] = zero_plane
        FYR[lt] = zero_plane
        for k in range(ITERS):
            V[k, lt, 0, Y0 : Y0 + ny] = zero_plane
            V[k, lt, nx + 1, Y0 : Y0 + ny] = zero_plane
            YR[k, 0, lt] = zero_plane
            YR[k, 1, lt] = zero_plane

    barrier = pltpu.get_barrier_semaphore()

    @pl.loop(1, N_GX)
    def _(d):
        pl.semaphore_signal(
            barrier, inc=1, device_id=(lax.rem(gx + d, N_GX), gy), device_id_type=MESH
        )

    has_up = gy < n_gy - 1
    has_down = gy > 0

    @pl.when(has_down)
    def _():
        pl.semaphore_signal(barrier, inc=1, device_id=(gx, gy - 1), device_id_type=MESH)

    @pl.when(has_up)
    def _():
        pl.semaphore_signal(barrier, inc=1, device_id=(gx, gy + 1), device_id_type=MESH)

    owners = [owner_ref[0, (4 * (b // 4)) * 16 + 4 * (b % 4)] for b in range(16)]
    for o in range(16):
        found = jnp.int32(0)
        for b in range(16):
            found = jnp.where(owners[b] == o, jnp.int32(b), found)
        box_of[o] = found

    sides = jnp.where(has_down, 1, 0) + jnp.where(has_up, 1, 0)
    pl.semaphore_wait(barrier, N_GX - 1 + sides)

    def remote(src, dst, send, recv, to_x, to_y):
        return pltpu.make_async_remote_copy(
            src_ref=src,
            dst_ref=dst,
            send_sem=send,
            recv_sem=recv,
            device_id=(to_x, to_y),
            device_id_type=MESH,
        )

    def guarded(pred, fn):
        @pl.when(pred)
        def _():
            fn()

    x_low, x_high = gx > 0, gx < N_GX - 1

    face_x = remote(FX.at[:, pl.ds(0, 1)], FXR, face_send.at[0], face_recv.at[0], gx - 1, gy)
    face_y = remote(FYP, FYR, face_send.at[1], face_recv.at[1], gx, gy - 1)
    fy_flat = FY.reshape(nl, nx * 40, LANES)

    def wait_load(which):
        for lt in range(nl):
            loads[lt][which].wait()

    wait_load(0)
    guarded(x_low, face_x.start)
    wait_load(1)
    for lt in range(nl):
        FYP[lt] = fy_flat[lt, pl.ds(0, nx, stride=40), :]
    guarded(has_down, face_y.start)

    lane = lax.broadcasted_iota(jnp.int32, (8, LANES), 1)
    first_lane, last_lane = lane == 0, lane == LANES - 1
    blank = jnp.zeros((8, LANES), jnp.float32)

    def z_lower(c):
        turned = [pltpu.roll(ci, 1, axis=1) for ci in c]
        return [
            jnp.where(first_lane, turned[i - 1] if i else blank, turned[i]) for i in range(nl)
        ]

    def z_upper(c):
        turned = [pltpu.roll(ci, LANES - 1, axis=1) for ci in c]
        return [
            jnp.where(last_lane, turned[i + 1] if i < nl - 1 else blank, turned[i])
            for i in range(nl)
        ]

    v_flat = V.reshape(ITERS, nl, (nx + 2) * 48, LANES)

    def halo_copies(k):
        rows = pl.ds(Y0, ny)
        down_x = remote(
            V.at[k, :, pl.ds(1, 1), rows],
            V.at[k, :, pl.ds(nx + 1, 1), rows],
            halo_send.at[k, 0],
            halo_recv.at[k, 0],
            gx - 1,
            gy,
        )
        up_x = remote(
            V.at[k, :, pl.ds(nx, 1), rows],
            V.at[k, :, pl.ds(0, 1), rows],
            halo_send.at[k, 1],
            halo_recv.at[k, 1],
            gx + 1,
            gy,
        )
        row_0, row_1 = (YX.at[k, side, :, pl.ds(8, nx)] for side in range(2))
        down_y = remote(row_0, YR.at[k, 1], halo_send.at[k, 2], halo_recv.at[k, 2], gx, gy - 1)
        up_y = remote(row_1, YR.at[k, 0], halo_send.at[k, 3], halo_recv.at[k, 3], gx, gy + 1)
        return down_x, up_x, down_y, up_y

    halos = [halo_copies(k) for k in range(ITERS)]

    def send_low_x(k):
        guarded(x_low, halos[k][0].start)

    def send_high_x(k):
        guarded(x_high, halos[k][1].start)

    def send_low_y(k):
        guarded(has_down, halos[k][2].start)

    def send_high_y(k):
        guarded(has_up, halos[k][3].start)

    def wait_halo(k):
        down_x, up_x, down_y, up_y = halos[k]
        guarded(x_low, down_x.wait_send)
        guarded(x_high, down_x.wait_recv)
        guarded(x_high, up_x.wait_send)
        guarded(x_low, up_x.wait_recv)
        guarded(has_down, down_y.wait_send)
        guarded(has_up, down_y.wait_recv)
        guarded(has_up, up_y.wait_send)
        guarded(has_down, up_y.wait_recv)

    def insert_ends(k):
        for lt in range(nl):
            for x in (0, nx - 1):
                at = pl.ds(x, 1)
                V[k, lt, x + 1, pl.ds(Y0 - 1, 1), :] = YR[k, 0, lt, at, :]
                V[k, lt, x + 1, pl.ds(Y0 + ny, 1), :] = YR[k, 1, lt, at, :]
            for side, y in ((0, 0), (1, ny - 1)):
                YX[k, side, lt, pl.ds(7, 1), :] = V[k, lt, 0, pl.ds(Y0 + y, 1), :]
                YX[k, side, lt, pl.ds(8 + nx, 1), :] = V[k, lt, nx + 1, pl.ds(Y0 + y, 1), :]

    def insert_rows(k):
        for lt in range(nl):
            v_flat[k, lt, pl.ds(48 + Y0 - 1, nx, stride=48), :] = YR[k, 0, lt]
            v_flat[k, lt, pl.ds(48 + Y0 + ny, nx, stride=48), :] = YR[k, 1, lt]

    def planes(body, lo, hi, tiles, unroll):
        def step(x, carry):
            body(x, tiles)
            return carry

        lax.fori_loop(lo, hi, step, 0, unroll=unroll)

    def first(x, tiles):
        for yt in tiles:
            rows = pl.ds(8 * yt, 8)
            fz = [FZ[lt, x, rows, :] for lt in range(nl)]
            fzu = z_upper(fz)
            for lt in range(nl):
                d = AL[lt, x, rows, :] + FX[lt, x, rows, :] + FX[lt, x + 1, rows, :]
                d = d + FY[lt, x, rows, :] + FY[lt, x, pl.ds(8 * yt + 1, 8), :]
                d = d + fz[lt] + fzu[lt]
                inv = 1.0 / d
                FZU[lt, x, rows, :] = fzu[lt]
                DG[lt, x, rows, :] = d
                INV[lt, x, rows, :] = inv
                V[0, lt, x + 1, pl.ds(Y0 + 8 * yt, 8), :] = inv * B[lt, x, rows, :] * (1.0 / theta)

    def gathered(k, x, yt):
        rows = pl.ds(8 * yt, 8)
        y = Y0 + 8 * yt
        c = [V[k, lt, x + 1, pl.ds(y, 8), :] for lt in range(nl)]
        low, high = z_lower(c), z_upper(c)
        t = []
        for lt in range(nl):
            s = B[lt, x, rows, :] + FX[lt, x, rows, :] * V[k, lt, x, pl.ds(y, 8), :]
            s = s + FX[lt, x + 1, rows, :] * V[k, lt, x + 2, pl.ds(y, 8), :]
            s = s + FY[lt, x, rows, :] * V[k, lt, x + 1, pl.ds(y - 1, 8), :]
            s = s + FY[lt, x, pl.ds(8 * yt + 1, 8), :] * V[k, lt, x + 1, pl.ds(y + 1, 8), :]
            s = s + FZ[lt, x, rows, :] * low[lt] + FZU[lt, x, rows, :] * high[lt]
            t.append(s)
        return t, c

    def sweep(k, c1, c2):
        def body(x, tiles):
            for yt in tiles:
                t, c = gathered(k, x, yt)
                rows = pl.ds(8 * yt, 8)
                y = pl.ds(Y0 + 8 * yt, 8)
                for lt in range(nl):
                    new = (1.0 + c1 - c2) * c[lt] + c2 * (INV[lt, x, rows, :] * t[lt])
                    if k > 0:
                        new = new - c1 * V[k - 1, lt, x + 1, y, :]
                    V[k + 1, lt, x + 1, y, :] = new
                    if k == ITERS - 2:
                        sol_ref[x, rows, lt * LANES : (lt + 1) * LANES] = new

        return body

    fx_flat = FX.reshape(nl, (nx + 1) * ny, LANES)
    b_flat, dg_flat, fz_flat, fzu_flat, inv_flat = (
        ref.reshape(nl, nx * ny, LANES) for ref in (B, DG, FZ, FZU, INV)
    )

    def pack_edges():
        for side, y in ((0, 0), (1, ny - 1)):
            for lt in range(nl):
                own, above = pl.ds(y, nx, stride=ny), pl.ds(ny + y, nx, stride=ny)
                EC[0, side, lt] = b_flat[lt, own, :]
                EC[1, side, lt] = fx_flat[lt, own, :]
                EC[2, side, lt] = fx_flat[lt, above, :]
                EC[3, side, lt] = fy_flat[lt, pl.ds(y, nx, stride=40), :]
                EC[4, side, lt] = fy_flat[lt, pl.ds(y + 1, nx, stride=40), :]
                EC[5, side, lt] = fz_flat[lt, own, :]
                EC[6, side, lt] = fzu_flat[lt, own, :]
                EC[7, side, lt] = inv_flat[lt, own, :]

    def edge_rows(k, c1, c2, side):
        inner = 1 if side == 0 else ny - 2
        for j in range(nx // 8):
            rows = pl.ds(8 * j, 8)
            c = [YX[k, side, lt, pl.ds(8 + 8 * j, 8), :] for lt in range(nl)]
            low, high = z_lower(c), z_upper(c)
            for lt in range(nl):

                def coef(i):
                    return EC[i, side, lt, rows, :]

                beyond = YR[k, side, lt, rows, :]
                within = v_flat[k, lt, pl.ds((1 + 8 * j) * 48 + Y0 + inner, 8, stride=48), :]
                y_low, y_high = (beyond, within) if side == 0 else (within, beyond)
                t = coef(0) + coef(1) * YX[k, side, lt, pl.ds(7 + 8 * j, 8), :]
                t = t + coef(2) * YX[k, side, lt, pl.ds(9 + 8 * j, 8), :]
                t = t + coef(3) * y_low
                t = t + coef(4) * y_high
                t = t + coef(5) * low[lt] + coef(6) * high[lt]
                new = (1.0 + c1 - c2) * c[lt] + c2 * (coef(7) * t)
                if k > 0:
                    new = new - c1 * YX[k - 1, side, lt, pl.ds(8 + 8 * j, 8), :]
                YX[k + 1, side, lt, pl.ds(8 + 8 * j, 8), :] = new

    row_i = lax.broadcasted_iota(jnp.int32, (LANES, LANES), 0)
    col_i = lax.broadcasted_iota(jnp.int32, (LANES, LANES), 1)
    groups = [(lane // 16) // d % 2 == 1 for d in (4, 2, 1)]

    def restrict(f, pairs, weight, even_only, first_x=0, last_x=16):
        def gather(X, carry):
            for lt in range(nl):
                SB[lt, pl.ds(pl.multiple_of(X * 16, 16), 16), :] = pairs(lt, X)
            return carry

        lax.fori_loop(first_x, last_x, gather, 0, unroll=4)
        for half in range(2):
            total = None
            for side in range(2):
                hit = row_i // 2 + 64 * side == col_i
                if even_only:
                    hit = hit & (row_i % 2 == 0)
                pick = jnp.where(hit, weight, 0.0).astype(jnp.float32).astype(jnp.bfloat16)
                rest = SB[2 * half + side, first_x * 16 : last_x * 16]
                for _ in range(3):
                    piece = rest.astype(jnp.bfloat16)
                    rest = rest - piece.astype(jnp.float32)
                    part = jnp.dot(piece, pick, preferred_element_type=jnp.float32)
                    total = part if total is None else total + part
            CB[half, first_x:last_x] = total.reshape(last_x - first_x, 16, LANES)

        for half in range(2):
            for yt in range(2):
                for xt in range(first_x // 8, last_x // 8):
                    a = [CB[half, xt * 8 + j, 8 * yt : 8 * yt + 8, :] for j in range(8)]
                    for d, odd in zip((4, 2, 1), groups):
                        b = list(a)
                        for j in range(8):
                            if j & d == 0:
                                lo, hi = a[j], a[j + d]
                                b[j] = jnp.where(odd, pltpu.roll(hi, 16 * d, axis=1), lo)
                                b[j + d] = jnp.where(
                                    odd, hi, pltpu.roll(lo, LANES - 16 * d, axis=1)
                                )
                        a = b
                    for j in range(8):
                        T[f, yt * 2 + xt, half * 2 + j // 4, j % 4] = a[j]

    def strided(ref, lt, x, start):
        return ref[lt, x, pl.ds(start, 16, stride=2), :]

    def four(ref):
        return lambda lt, X: (
            strided(ref, lt, 2 * X, 0)
            + strided(ref, lt, 2 * X, 1)
            + strided(ref, lt, 2 * X + 1, 0)
            + strided(ref, lt, 2 * X + 1, 1)
        )

    spread = (RA, RB, RC, RD, RE)

    def stage_one(f):
        copies = []
        for j in range(1, 4):
            q = lax.rem(bx + j, 4)
            copies.append(
                remote(
                    T.at[f, q],
                    spread[f].at[pl.ds(bx * 4, 4)],
                    one_send.at[f, j],
                    one_recv.at[f, j],
                    q * 4 + r,
                    gy,
                )
            )
        own = pltpu.make_async_copy(T.at[f, bx], spread[f].at[pl.ds(bx * 4, 4)], one_local.at[f])
        return copies, own

    first_stage = [stage_one(f) for f in range(4)]

    def start_one(f):
        copies, own = first_stage[f]
        for c in copies:
            c.start()
        own.start()

    def wait_one(f):
        copies, own = first_stage[f]
        for c in copies:
            c.wait()
        own.wait()

    mine = RE.at[pl.ds(bx * 4, 4)]

    def residual_quarter(q, source):
        return remote(
            T.at[4, q], mine, one_send.at[4, q], one_recv.at[4, source], q * 4 + r, gy
        )

    own_quarter = pltpu.make_async_copy(T.at[4, bx], mine, one_local.at[4])

    def start_residual(q):
        guarded(bx != q, residual_quarter(q, bx).start)
        guarded(bx == q, own_quarter.start)

    def wait_residual():
        for q in range(4):
            guarded(bx != q, residual_quarter(q, bx).wait_send)
        for source in range(4):
            guarded(bx != source, residual_quarter(0, source).wait_recv)
        own_quarter.wait()

    yt, xt = bx // 2, bx % 2
    out_rows = pl.ds(pl.multiple_of(r * 4, 4), 4)
    out_y = pl.ds(pl.multiple_of(yt * 8, 8), 8)
    out_cols = pl.ds(pl.multiple_of(xt * LANES, LANES), LANES)

    def landing(f):
        if f == 4:
            return cres_ref.at[out_rows, out_y, out_cols]
        return ccoef_ref.at[f, out_rows, out_y, out_cols]

    def two_copy(f, d):
        o = lax.rem(gx + d, N_GX)
        return remote(S2.at[f, o], landing(f), two_send.at[f, d], two_recv.at[f, d], o, gy)

    def two_own(f):
        return pltpu.make_async_copy(S2.at[f, gx], landing(f), two_local.at[f])

    def start_two(f):
        @pl.loop(0, N_GX - 1)
        def _(i):
            d = lax.rem(i + 5, N_GX - 1) + 1
            o = lax.rem(gx + d, N_GX)
            S2[f, o] = spread[f][box_of[o]]
            two_copy(f, d).start()

        S2[f, gx] = spread[f][box_of[gx]]
        two_own(f).start()

    def wait_two(f):
        @pl.loop(1, N_GX)
        def _(d):
            two_copy(f, d).wait()

        two_own(f).wait()

    def advance(k):
        body = sweep(k, *steps[k])
        insert_ends(k)
        body(0, (0, 1, 2, 3))
        send_low_x(k + 1)
        body(nx - 1, (0, 1, 2, 3))
        send_high_x(k + 1)
        edge_rows(k, *steps[k], 0)
        send_low_y(k + 1)
        edge_rows(k, *steps[k], 1)
        send_high_y(k + 1)
        insert_rows(k)
        planes(body, 1, nx - 1, (0, 1, 2, 3), 5)

    def restrict_y():
        def pairs(lt, X):
            return strided(FY, lt, 2 * X, 0) + strided(FY, lt, 2 * X + 1, 0)

        restrict(2, pairs, 0.25, False)

    def restrict_x():
        def pairs(lt, X):
            return strided(FX, lt, 2 * X, 0) + strided(FX, lt, 2 * X, 1)

        restrict(1, pairs, 0.25, False)

    restrict_y()
    start_one(2)
    for which in (2, 3, 4):
        wait_load(which)
    for lt in range(nl):
        fy_flat[lt, pl.ds(ny, nx, stride=40), :] = zero_plane
    planes(first, 0, nx, (0, 1, 2, 3), 4)
    guarded(x_high, face_x.wait_recv)
    guarded(x_low, face_x.wait_send)
    guarded(has_up, face_y.wait_recv)
    guarded(has_down, face_y.wait_send)
    for lt in range(nl):
        FX[lt, nx] = FXR[lt, 0]
        fy_flat[lt, pl.ds(ny, nx, stride=40), :] = FYR[lt]
        last_row = pl.ds(ny - 1, nx, stride=ny)
        d = dg_flat[lt, last_row, :] + FYR[lt]
        inv = 1.0 / d
        dg_flat[lt, last_row, :] = d
        inv_flat[lt, last_row, :] = inv
        v_flat[0, lt, pl.ds(48 + Y0 + ny - 1, nx, stride=48), :] = (
            inv * b_flat[lt, last_row, :] * (1.0 / theta)
        )
    first(nx - 1, (0, 1, 2, 3))
    send_low_x(0)
    send_high_x(0)
    for lt in range(nl):
        YX[0, 0, lt, 8 : 8 + nx] = v_flat[0, lt, pl.ds(48 + Y0, nx, stride=48), :]
        YX[0, 1, lt, 8 : 8 + nx] = v_flat[0, lt, pl.ds(48 + Y0 + ny - 1, nx, stride=48), :]
    send_low_y(0)
    send_high_y(0)
    restrict(3, four(FZ), 0.25, True)
    start_one(3)
    restrict(0, four(AL), 0.125, False)
    start_one(0)
    pack_edges()
    wait_halo(0)
    advance(0)
    restrict_x()
    start_one(1)
    wait_one(2)
    start_two(2)
    wait_halo(1)
    advance(1)
    wait_one(3)
    start_two(3)
    wait_halo(2)
    advance(2)
    wait_one(0)
    start_two(0)

    def last(X, tiles):
        for yt_ in tiles:
            rows = pl.ds(8 * yt_, 8)
            acc = None
            for a in range(2):
                x = 2 * X + a
                t, c = gathered(3, x, yt_)
                res = [t[lt] - DG[lt, x, rows, :] * c[lt] for lt in range(nl)]
                acc = res if acc is None else [p + q for p, q in zip(acc, res)]
            for lt in range(nl):
                RES[lt, X, rows, :] = acc[lt]

    def restrict_residual(lo, hi):
        def pairs(lt, X):
            return strided(RES, lt, X, 0) + strided(RES, lt, X, 1)

        restrict(4, pairs, 0.125, False, lo, hi)

    planes(last, 1, 15, (1, 2), 2)
    wait_halo(3)
    insert_rows(3)
    last(0, (0, 1, 2, 3))
    planes(last, 1, 8, (0, 3), 7)
    restrict_residual(0, 8)
    start_residual(0)
    start_residual(2)
    planes(last, 8, 15, (0, 3), 7)
    last(15, (0, 1, 2, 3))
    restrict_residual(8, 16)
    start_residual(1)
    start_residual(3)
    wait_one(1)
    start_two(1)
    wait_residual()
    start_two(4)
    for f in range(5):
        wait_two(f)


def write_out(sol_ref, cres_ref, ccoef_ref, sol_hbm, cres_hbm, ccoef_hbm, sem):
    copies = []
    for i in range(4):
        part = pl.ds(8 * i, 8)
        copies.append(pltpu.make_async_copy(sol_ref.at[part], sol_hbm.at[part], sem.at[i]))
    copies.append(pltpu.make_async_copy(ccoef_ref, ccoef_hbm, sem.at[4]))
    copies.append(pltpu.make_async_copy(cres_ref, cres_hbm, sem.at[5]))
    for c in copies:
        c.start()
    for c in copies:
        c.wait()


def local(n_gy, right_side, alpha_coef, face_coef, owner_map):
    f32 = jnp.float32
    vmem = pltpu.VMEM
    dma = pltpu.SemaphoreType.DMA
    hbm = pl.BlockSpec(memory_space=pl.ANY)
    cells = vmem((4, 32, 32, LANES), f32)
    on_chip = pl.BlockSpec(memory_space=pltpu.VMEM)
    sol, cres, ccoef = pl.pallas_call(
        functools.partial(kernel, n_gy),
        out_shape=(
            vmem((32, 32, 512), f32),
            vmem((16, 16, 256), f32),
            vmem((4, 16, 16, 256), f32),
        ),
        in_specs=[pl.BlockSpec(memory_space=pltpu.SMEM), hbm, hbm, hbm],
        out_specs=(on_chip, on_chip, on_chip),
        scratch_shapes=[
            cells,
            cells,
            vmem((4, 33, 32, LANES), f32),
            vmem((4, 32, 40, LANES), f32),
            cells,
            cells,
            cells,
            cells,
            vmem((ITERS, 4, 34, 48, LANES), f32),
            vmem((4, 16, 32, LANES), f32),
            vmem((ITERS, 2, 4, 48, LANES), f32),
            vmem((ITERS, 2, 4, 32, LANES), f32),
            vmem((8, 2, 4, 32, LANES), f32),
            vmem((4, 32, LANES), f32),
            vmem((4, 32, LANES), f32),
            vmem((4, 1, 32, LANES), f32),
            vmem((4, 256, LANES), f32),
            vmem((2, 16, 16, LANES), f32),
            vmem((5, 4, 4, 4, 8, LANES), f32),
            *[vmem((16, 4, 8, LANES), f32)] * 5,
            vmem((5, 16, 4, 8, LANES), f32),
            pltpu.SMEM((16,), jnp.int32),
            dma((5, 4)),
            dma((2,)),
            dma((2,)),
            dma((ITERS, 4)),
            dma((ITERS, 4)),
            dma((5, 4)),
            dma((5, 4)),
            dma((5,)),
            dma((5, 16)),
            dma((5, 16)),
            dma((5,)),
        ],
        compiler_params=pltpu.CompilerParams(
            collective_id=0, has_side_effects=True, vmem_limit_bytes=60 << 20
        ),
        name="smooth_and_restrict",
    )(owner_map, right_side, alpha_coef, face_coef)
    arrays = (sol, cres, ccoef)
    return pl.pallas_call(
        write_out,
        out_shape=tuple(jax.ShapeDtypeStruct(x.shape, f32) for x in arrays),
        in_specs=[on_chip] * 3,
        out_specs=(hbm,) * 3,
        scratch_shapes=[dma((6,))],
        compiler_params=pltpu.CompilerParams(vmem_limit_bytes=1 << 20),
        name="write_out",
    )(*arrays)


def solution(mesh):
    return jax.shard_map(
        functools.partial(local, mesh.shape["gy"]),
        mesh=mesh,
        in_specs=(
            P("gx", "gy", None),
            P("gx", "gy", None),
            P(None, "gx", "gy", None),
            P("gy", None),
        ),
        out_specs=(P("gx", "gy", None), P("gx", "gy", None), P(None, "gx", "gy", None)),
        check_vma=False,
    )
```

```python
import functools

import jax
import jax.numpy as jnp
from jax import lax
from jax.experimental import pallas as pl
from jax.experimental.pallas import tpu as pltpu
from jax.sharding import PartitionSpec as P

ITERS = 4
CHEB_HIGH = 2.0
CHEB_LOW = 0.25

MESH = pl.DeviceIdType.MESH
LANES = 128
N_GX = 16
Y0 = 8


def chebyshev_steps():
    theta = (CHEB_HIGH + CHEB_LOW) / 2.0
    delta = (CHEB_HIGH - CHEB_LOW) / 2.0
    sigma = theta / delta
    rho = 1.0 / sigma
    steps = []
    for _ in range(ITERS - 1):
        rho_next = 1.0 / (2.0 * sigma - rho)
        steps.append((rho_next * rho, 2.0 * rho_next / delta))
        rho = rho_next
    return theta, steps


def kernel(
    n_gy,
    owner_ref,
    b_hbm,
    alpha_hbm,
    face_hbm,
    sol_ref,
    cres_ref,
    ccoef_ref,
    B,
    AL,
    FX,
    FY,
    FZ,
    FZU,
    INV,
    DG,
    V,
    RES,
    YX,
    YR,
    EC,
    FYP,
    FYR,
    FXR,
    SB,
    CB,
    T,
    RA,
    RB,
    RC,
    RD,
    RE,
    S2,
    box_of,
    load_sem,
    face_send,
    face_recv,
    halo_send,
    halo_recv,
    one_send,
    one_recv,
    one_local,
    two_send,
    two_recv,
    two_local,
):
    nx, ny = 32, 32
    nl = 4
    gx = lax.axis_index("gx")
    gy = lax.axis_index("gy")
    bx, r = gx // 4, gx % 4
    theta, steps = chebyshev_steps()

    def load(src, dst, which, lt):
        return pltpu.make_async_copy(src, dst, load_sem.at[which, lt])

    loads = []
    for lt in range(nl):
        cols = pl.ds(lt * LANES, LANES)
        loads.append(
            [
                load(face_hbm.at[0, :, :, cols], FX.at[lt, pl.ds(0, nx)], 0, lt),
                load(face_hbm.at[1, :, :, cols], FY.at[lt, :, pl.ds(0, ny)], 1, lt),
                load(face_hbm.at[2, :, :, cols], FZ.at[lt], 2, lt),
                load(alpha_hbm.at[:, :, cols], AL.at[lt], 3, lt),
                load(b_hbm.at[:, :, cols], B.at[lt], 4, lt),
            ]
        )
    for which in range(5):
        for lt in range(nl):
            loads[lt][which].start()

    zero_plane = jnp.zeros((ny, LANES), jnp.float32)
    for lt in range(nl):
        FX[lt, nx] = zero_plane
        FXR[lt, 0] = zero_plane
        FYR[lt] = zero_plane
        for k in range(ITERS):
            V[k, lt, 0, Y0 : Y0 + ny] = zero_plane
            V[k, lt, nx + 1, Y0 : Y0 + ny] = zero_plane
            YR[k, 0, lt] = zero_plane
            YR[k, 1, lt] = zero_plane

    v_flat = V.reshape(ITERS, nl, (nx + 2) * 48, LANES)
    for lt in range(nl):
        v_flat[ITERS - 1, lt, pl.ds(48 + Y0 - 1, nx, stride=48), :] = zero_plane
        v_flat[ITERS - 1, lt, pl.ds(48 + Y0 + ny, nx, stride=48), :] = zero_plane

    barrier = pltpu.get_barrier_semaphore()

    @pl.loop(1, N_GX)
    def _(d):
        pl.semaphore_signal(
            barrier, inc=1, device_id=(lax.rem(gx + d, N_GX), gy), device_id_type=MESH
        )

    has_up = gy < n_gy - 1
    has_down = gy > 0

    @pl.when(has_down)
    def _():
        pl.semaphore_signal(barrier, inc=1, device_id=(gx, gy - 1), device_id_type=MESH)

    @pl.when(has_up)
    def _():
        pl.semaphore_signal(barrier, inc=1, device_id=(gx, gy + 1), device_id_type=MESH)

    owners = [owner_ref[0, (4 * (b // 4)) * 16 + 4 * (b % 4)] for b in range(16)]
    for o in range(16):
        found = jnp.int32(0)
        for b in range(16):
            found = jnp.where(owners[b] == o, jnp.int32(b), found)
        box_of[o] = found

    sides = jnp.where(has_down, 1, 0) + jnp.where(has_up, 1, 0)
    pl.semaphore_wait(barrier, N_GX - 1 + sides)

    def remote(src, dst, send, recv, to_x, to_y):
        return pltpu.make_async_remote_copy(
            src_ref=src,
            dst_ref=dst,
            send_sem=send,
            recv_sem=recv,
            device_id=(to_x, to_y),
            device_id_type=MESH,
        )

    def guarded(pred, fn):
        @pl.when(pred)
        def _():
            fn()

    x_low, x_high = gx > 0, gx < N_GX - 1

    face_x = remote(FX.at[:, pl.ds(0, 1)], FXR, face_send.at[0], face_recv.at[0], gx - 1, gy)
    face_y = remote(FYP, FYR, face_send.at[1], face_recv.at[1], gx, gy - 1)
    fy_flat = FY.reshape(nl, nx * 40, LANES)

    def wait_load(which):
        for lt in range(nl):
            loads[lt][which].wait()

    wait_load(0)
    guarded(x_low, face_x.start)
    wait_load(1)
    for lt in range(nl):
        FYP[lt] = fy_flat[lt, pl.ds(0, nx, stride=40), :]
    guarded(has_down, face_y.start)

    lane = lax.broadcasted_iota(jnp.int32, (8, LANES), 1)
    first_lane, last_lane = lane == 0, lane == LANES - 1
    blank = jnp.zeros((8, LANES), jnp.float32)

    def z_lower(c):
        turned = [pltpu.roll(ci, 1, axis=1) for ci in c]
        return [
            jnp.where(first_lane, turned[i - 1] if i else blank, turned[i]) for i in range(nl)
        ]

    def z_upper(c):
        turned = [pltpu.roll(ci, LANES - 1, axis=1) for ci in c]
        return [
            jnp.where(last_lane, turned[i + 1] if i < nl - 1 else blank, turned[i])
            for i in range(nl)
        ]

    def halo_copies(k):
        rows = pl.ds(Y0, ny)
        down_x = remote(
            V.at[k, :, pl.ds(1, 1), rows],
            V.at[k, :, pl.ds(nx + 1, 1), rows],
            halo_send.at[k, 0],
            halo_recv.at[k, 0],
            gx - 1,
            gy,
        )
        up_x = remote(
            V.at[k, :, pl.ds(nx, 1), rows],
            V.at[k, :, pl.ds(0, 1), rows],
            halo_send.at[k, 1],
            halo_recv.at[k, 1],
            gx + 1,
            gy,
        )
        row_0, row_1 = (YX.at[k, side, :, pl.ds(8, nx)] for side in range(2))
        down_y = remote(row_0, YR.at[k, 1], halo_send.at[k, 2], halo_recv.at[k, 2], gx, gy - 1)
        up_y = remote(row_1, YR.at[k, 0], halo_send.at[k, 3], halo_recv.at[k, 3], gx, gy + 1)
        return down_x, up_x, down_y, up_y

    halos = [halo_copies(k) for k in range(ITERS)]

    def send_low_x(k):
        guarded(x_low, halos[k][0].start)

    def send_high_x(k):
        guarded(x_high, halos[k][1].start)

    def send_low_y(k):
        guarded(has_down, halos[k][2].start)

    def send_high_y(k):
        guarded(has_up, halos[k][3].start)

    def wait_halo(k):
        down_x, up_x, down_y, up_y = halos[k]
        guarded(x_low, down_x.wait_send)
        guarded(x_high, down_x.wait_recv)
        guarded(x_high, up_x.wait_send)
        guarded(x_low, up_x.wait_recv)
        guarded(has_down, down_y.wait_send)
        guarded(has_up, down_y.wait_recv)
        guarded(has_up, up_y.wait_send)
        guarded(has_down, up_y.wait_recv)

    def insert_ends(k):
        for lt in range(nl):
            for x in (0, nx - 1):
                at = pl.ds(x, 1)
                V[k, lt, x + 1, pl.ds(Y0 - 1, 1), :] = YR[k, 0, lt, at, :]
                V[k, lt, x + 1, pl.ds(Y0 + ny, 1), :] = YR[k, 1, lt, at, :]
            for side, y in ((0, 0), (1, ny - 1)):
                YX[k, side, lt, pl.ds(7, 1), :] = V[k, lt, 0, pl.ds(Y0 + y, 1), :]
                YX[k, side, lt, pl.ds(8 + nx, 1), :] = V[k, lt, nx + 1, pl.ds(Y0 + y, 1), :]

    def insert_rows(k):
        for lt in range(nl):
            v_flat[k, lt, pl.ds(48 + Y0 - 1, nx, stride=48), :] = YR[k, 0, lt]
            v_flat[k, lt, pl.ds(48 + Y0 + ny, nx, stride=48), :] = YR[k, 1, lt]

    def planes(body, lo, hi, tiles, unroll):
        def step(x, carry):
            body(x, tiles)
            return carry

        lax.fori_loop(lo, hi, step, 0, unroll=unroll)

    def first(x, tiles):
        for yt in tiles:
            rows = pl.ds(8 * yt, 8)
            fz = [FZ[lt, x, rows, :] for lt in range(nl)]
            fzu = z_upper(fz)
            for lt in range(nl):
                d = AL[lt, x, rows, :] + FX[lt, x, rows, :] + FX[lt, x + 1, rows, :]
                d = d + FY[lt, x, rows, :] + FY[lt, x, pl.ds(8 * yt + 1, 8), :]
                d = d + fz[lt] + fzu[lt]
                inv = 1.0 / d
                FZU[lt, x, rows, :] = fzu[lt]
                DG[lt, x, rows, :] = d
                INV[lt, x, rows, :] = inv
                V[0, lt, x + 1, pl.ds(Y0 + 8 * yt, 8), :] = inv * B[lt, x, rows, :] * (1.0 / theta)

    def gathered(k, x, yt, low_x=True, high_x=True):
        rows = pl.ds(8 * yt, 8)
        y = Y0 + 8 * yt
        c = [V[k, lt, x + 1, pl.ds(y, 8), :] for lt in range(nl)]
        low, high = z_lower(c), z_upper(c)
        t = []
        for lt in range(nl):
            s = B[lt, x, rows, :]
            if low_x:
                s = s + FX[lt, x, rows, :] * V[k, lt, x, pl.ds(y, 8), :]
            if high_x:
                s = s + FX[lt, x + 1, rows, :] * V[k, lt, x + 2, pl.ds(y, 8), :]
            s = s + FY[lt, x, rows, :] * V[k, lt, x + 1, pl.ds(y - 1, 8), :]
            s = s + FY[lt, x, pl.ds(8 * yt + 1, 8), :] * V[k, lt, x + 1, pl.ds(y + 1, 8), :]
            s = s + FZ[lt, x, rows, :] * low[lt] + FZU[lt, x, rows, :] * high[lt]
            t.append(s)
        return t, c

    def sweep(k, c1, c2):
        def body(x, tiles):
            for yt in tiles:
                t, c = gathered(k, x, yt)
                rows = pl.ds(8 * yt, 8)
                y = pl.ds(Y0 + 8 * yt, 8)
                for lt in range(nl):
                    new = (1.0 + c1 - c2) * c[lt] + c2 * (INV[lt, x, rows, :] * t[lt])
                    if k > 0:
                        new = new - c1 * V[k - 1, lt, x + 1, y, :]
                    V[k + 1, lt, x + 1, y, :] = new
                    if k == ITERS - 2:
                        sol_ref[x, rows, lt * LANES : (lt + 1) * LANES] = new

        return body

    fx_flat = FX.reshape(nl, (nx + 1) * ny, LANES)
    b_flat, dg_flat, fz_flat, fzu_flat, inv_flat = (
        ref.reshape(nl, nx * ny, LANES) for ref in (B, DG, FZ, FZU, INV)
    )

    def pack_edges():
        for side, y in ((0, 0), (1, ny - 1)):
            for lt in range(nl):
                own, above = pl.ds(y, nx, stride=ny), pl.ds(ny + y, nx, stride=ny)
                EC[0, side, lt] = b_flat[lt, own, :]
                EC[1, side, lt] = fx_flat[lt, own, :]
                EC[2, side, lt] = fx_flat[lt, above, :]
                EC[3, side, lt] = fy_flat[lt, pl.ds(y, nx, stride=40), :]
                EC[4, side, lt] = fy_flat[lt, pl.ds(y + 1, nx, stride=40), :]
                EC[5, side, lt] = fz_flat[lt, own, :]
                EC[6, side, lt] = fzu_flat[lt, own, :]
                EC[7, side, lt] = inv_flat[lt, own, :]

    def edge_rows(k, c1, c2, side):
        inner = 1 if side == 0 else ny - 2
        for j in range(nx // 8):
            rows = pl.ds(8 * j, 8)
            c = [YX[k, side, lt, pl.ds(8 + 8 * j, 8), :] for lt in range(nl)]
            low, high = z_lower(c), z_upper(c)
            for lt in range(nl):

                def coef(i):
                    return EC[i, side, lt, rows, :]

                beyond = YR[k, side, lt, rows, :]
                within = v_flat[k, lt, pl.ds((1 + 8 * j) * 48 + Y0 + inner, 8, stride=48), :]
                y_low, y_high = (beyond, within) if side == 0 else (within, beyond)
                t = coef(0) + coef(1) * YX[k, side, lt, pl.ds(7 + 8 * j, 8), :]
                t = t + coef(2) * YX[k, side, lt, pl.ds(9 + 8 * j, 8), :]
                t = t + coef(3) * y_low
                t = t + coef(4) * y_high
                t = t + coef(5) * low[lt] + coef(6) * high[lt]
                new = (1.0 + c1 - c2) * c[lt] + c2 * (coef(7) * t)
                if k > 0:
                    new = new - c1 * YX[k - 1, side, lt, pl.ds(8 + 8 * j, 8), :]
                YX[k + 1, side, lt, pl.ds(8 + 8 * j, 8), :] = new

    row_i = lax.broadcasted_iota(jnp.int32, (LANES, LANES), 0)
    col_i = lax.broadcasted_iota(jnp.int32, (LANES, LANES), 1)
    groups = [(lane // 16) // d % 2 == 1 for d in (4, 2, 1)]

    def gather_pairs(pairs):
        def gather(X, carry):
            for lt in range(nl):
                SB[lt, pl.ds(pl.multiple_of(X * 16, 16), 16), :] = pairs(lt, X)
            return carry

        lax.fori_loop(0, 16, gather, 0, unroll=4)

    def restrict(f, pairs, weight, even_only):
        gather_pairs(pairs)
        to_tiles(f, weight, even_only)

    def to_tiles(f, weight, even_only):
        for half in range(2):
            total = None
            for side in range(2):
                hit = row_i // 2 + 64 * side == col_i
                if even_only:
                    hit = hit & (row_i % 2 == 0)
                pick = jnp.where(hit, weight, 0.0).astype(jnp.float32).astype(jnp.bfloat16)
                rest = SB[2 * half + side]
                for _ in range(3):
                    piece = rest.astype(jnp.bfloat16)
                    rest = rest - piece.astype(jnp.float32)
                    part = jnp.dot(piece, pick, preferred_element_type=jnp.float32)
                    total = part if total is None else total + part
            CB[half] = total.reshape(16, 16, LANES)

        for half in range(2):
            for yt in range(2):
                for xt in range(2):
                    a = [CB[half, xt * 8 + j, 8 * yt : 8 * yt + 8, :] for j in range(8)]
                    for d, odd in zip((4, 2, 1), groups):
                        b = list(a)
                        for j in range(8):
                            if j & d == 0:
                                lo, hi = a[j], a[j + d]
                                b[j] = jnp.where(odd, pltpu.roll(hi, 16 * d, axis=1), lo)
                                b[j + d] = jnp.where(
                                    odd, hi, pltpu.roll(lo, LANES - 16 * d, axis=1)
                                )
                        a = b
                    for j in range(8):
                        T[f, yt * 2 + xt, half * 2 + j // 4, j % 4] = a[j]

    def strided(ref, lt, x, start):
        return ref[lt, x, pl.ds(start, 16, stride=2), :]

    def four(ref):
        return lambda lt, X: (
            strided(ref, lt, 2 * X, 0)
            + strided(ref, lt, 2 * X, 1)
            + strided(ref, lt, 2 * X + 1, 0)
            + strided(ref, lt, 2 * X + 1, 1)
        )

    spread = (RA, RB, RC, RD, RE)

    def stage_one(f):
        copies = []
        for j in range(1, 4):
            q = lax.rem(bx + j, 4)
            copies.append(
                remote(
                    T.at[f, q],
                    spread[f].at[pl.ds(bx * 4, 4)],
                    one_send.at[f, j],
                    one_recv.at[f, j],
                    q * 4 + r,
                    gy,
                )
            )
        own = pltpu.make_async_copy(T.at[f, bx], spread[f].at[pl.ds(bx * 4, 4)], one_local.at[f])
        return copies, own

    first_stage = [stage_one(f) for f in range(4)]

    def start_one(f):
        copies, own = first_stage[f]
        for c in copies:
            c.start()
        own.start()

    def wait_one(f):
        copies, own = first_stage[f]
        for c in copies:
            c.wait()
        own.wait()

    mine = RE.at[pl.ds(bx * 4, 4)]

    def residual_quarter(q, source):
        return remote(
            T.at[4, q], mine, one_send.at[4, q], one_recv.at[4, source], q * 4 + r, gy
        )

    own_quarter = pltpu.make_async_copy(T.at[4, bx], mine, one_local.at[4])

    def start_residual(q):
        guarded(bx != q, residual_quarter(q, bx).start)
        guarded(bx == q, own_quarter.start)

    def wait_residual():
        for q in range(4):
            guarded(bx != q, residual_quarter(q, bx).wait_send)
        for source in range(4):
            guarded(bx != source, residual_quarter(0, source).wait_recv)
        own_quarter.wait()

    yt, xt = bx // 2, bx % 2
    out_rows = pl.ds(pl.multiple_of(r * 4, 4), 4)
    out_y = pl.ds(pl.multiple_of(yt * 8, 8), 8)
    out_cols = pl.ds(pl.multiple_of(xt * LANES, LANES), LANES)

    def landing(f):
        if f == 4:
            return cres_ref.at[out_rows, out_y, out_cols]
        return ccoef_ref.at[f, out_rows, out_y, out_cols]

    def two_copy(f, d):
        o = lax.rem(gx + d, N_GX)
        return remote(S2.at[f, o], landing(f), two_send.at[f, d], two_recv.at[f, d], o, gy)

    def two_own(f):
        return pltpu.make_async_copy(S2.at[f, gx], landing(f), two_local.at[f])

    def start_two(f):
        @pl.loop(0, N_GX - 1)
        def _(i):
            d = lax.rem(i + 5, N_GX - 1) + 1
            o = lax.rem(gx + d, N_GX)
            S2[f, o] = spread[f][box_of[o]]
            two_copy(f, d).start()

        S2[f, gx] = spread[f][box_of[gx]]
        two_own(f).start()

    def wait_two(f):
        @pl.loop(1, N_GX)
        def _(d):
            two_copy(f, d).wait()

        two_own(f).wait()

    def advance(k):
        body = sweep(k, *steps[k])
        insert_ends(k)
        body(0, (0, 1, 2, 3))
        send_low_x(k + 1)
        body(nx - 1, (0, 1, 2, 3))
        send_high_x(k + 1)
        edge_rows(k, *steps[k], 0)
        send_low_y(k + 1)
        edge_rows(k, *steps[k], 1)
        send_high_y(k + 1)
        insert_rows(k)
        planes(body, 1, nx - 1, (0, 1, 2, 3), 5)

    def restrict_y():
        def pairs(lt, X):
            return strided(FY, lt, 2 * X, 0) + strided(FY, lt, 2 * X + 1, 0)

        restrict(2, pairs, 0.25, False)

    def restrict_x():
        def pairs(lt, X):
            return strided(FX, lt, 2 * X, 0) + strided(FX, lt, 2 * X, 1)

        restrict(1, pairs, 0.25, False)

    restrict_y()
    start_one(2)
    for which in (2, 3, 4):
        wait_load(which)
    for lt in range(nl):
        fy_flat[lt, pl.ds(ny, nx, stride=40), :] = zero_plane
    planes(first, 0, nx, (0, 1, 2, 3), 4)
    guarded(x_high, face_x.wait_recv)
    guarded(x_low, face_x.wait_send)
    guarded(has_up, face_y.wait_recv)
    guarded(has_down, face_y.wait_send)
    for lt in range(nl):
        FX[lt, nx] = FXR[lt, 0]
        fy_flat[lt, pl.ds(ny, nx, stride=40), :] = FYR[lt]
        last_row = pl.ds(ny - 1, nx, stride=ny)
        d = dg_flat[lt, last_row, :] + FYR[lt]
        inv = 1.0 / d
        dg_flat[lt, last_row, :] = d
        inv_flat[lt, last_row, :] = inv
        v_flat[0, lt, pl.ds(48 + Y0 + ny - 1, nx, stride=48), :] = (
            inv * b_flat[lt, last_row, :] * (1.0 / theta)
        )
    first(nx - 1, (0, 1, 2, 3))
    send_low_x(0)
    send_high_x(0)
    for lt in range(nl):
        YX[0, 0, lt, 8 : 8 + nx] = v_flat[0, lt, pl.ds(48 + Y0, nx, stride=48), :]
        YX[0, 1, lt, 8 : 8 + nx] = v_flat[0, lt, pl.ds(48 + Y0 + ny - 1, nx, stride=48), :]
    send_low_y(0)
    send_high_y(0)
    restrict(3, four(FZ), 0.25, True)
    start_one(3)
    restrict(0, four(AL), 0.125, False)
    start_one(0)
    pack_edges()
    wait_halo(0)
    advance(0)
    restrict_x()
    start_one(1)
    wait_one(2)
    start_two(2)
    wait_halo(1)
    advance(1)
    wait_one(3)
    start_two(3)
    wait_halo(2)
    advance(2)

    def last(X, tiles, low_x=True, high_x=True):
        for yt_ in tiles:
            rows = pl.ds(8 * yt_, 8)
            acc = None
            for a in range(2):
                x = 2 * X + a
                t, c = gathered(3, x, yt_, low_x or a == 1, high_x or a == 0)
                res = [t[lt] - DG[lt, x, rows, :] * c[lt] for lt in range(nl)]
                acc = res if acc is None else [p + q for p, q in zip(acc, res)]
            for lt in range(nl):
                RES[lt, X, rows, :] = acc[lt]

    planes(last, 1, 15, (0, 1, 2, 3), 2)
    last(0, (0, 1, 2, 3), low_x=False)
    last(15, (0, 1, 2, 3), high_x=False)
    gather_pairs(lambda lt, X: strided(RES, lt, X, 0) + strided(RES, lt, X, 1))
    wait_one(0)
    start_two(0)
    wait_halo(3)
    rows = pl.ds(Y0, ny)
    for lt in range(nl):
        RES[lt, 0] = EC[3, 0, lt] * YR[3, 0, lt]
        RES[lt, 1] = EC[4, 1, lt] * YR[3, 1, lt]
        RES[lt, 2] = FX[lt, 0] * V[3, lt, 0, rows, :]
        RES[lt, 3] = FX[lt, nx] * V[3, lt, nx + 1, rows, :]
    for lt in range(nl):
        for i, cells_ in enumerate((pl.ds(0, 16, stride=16), pl.ds(15, 16, stride=16))):
            SB[lt, cells_, :] = SB[lt, cells_, :] + (strided(RES, lt, i, 0) + strided(RES, lt, i, 1))
    for lt in range(nl):
        for i, cells_ in ((2, pl.ds(0, 16)), (3, pl.ds(240, 16))):
            SB[lt, cells_, :] = SB[lt, cells_, :] + (strided(RES, lt, i, 0) + strided(RES, lt, i, 1))
    to_tiles(4, 0.125, False)
    for q in range(4):
        start_residual(q)
    wait_one(1)
    start_two(1)
    wait_residual()
    start_two(4)
    for f in range(5):
        wait_two(f)


def write_out(sol_ref, cres_ref, ccoef_ref, sol_hbm, cres_hbm, ccoef_hbm, sem):
    copies = []
    for i in range(4):
        part = pl.ds(8 * i, 8)
        copies.append(pltpu.make_async_copy(sol_ref.at[part], sol_hbm.at[part], sem.at[i]))
    copies.append(pltpu.make_async_copy(ccoef_ref, ccoef_hbm, sem.at[4]))
    copies.append(pltpu.make_async_copy(cres_ref, cres_hbm, sem.at[5]))
    for c in copies:
        c.start()
    for c in copies:
        c.wait()


def local(n_gy, right_side, alpha_coef, face_coef, owner_map):
    f32 = jnp.float32
    vmem = pltpu.VMEM
    dma = pltpu.SemaphoreType.DMA
    hbm = pl.BlockSpec(memory_space=pl.ANY)
    cells = vmem((4, 32, 32, LANES), f32)
    on_chip = pl.BlockSpec(memory_space=pltpu.VMEM)
    sol, cres, ccoef = pl.pallas_call(
        functools.partial(kernel, n_gy),
        out_shape=(
            vmem((32, 32, 512), f32),
            vmem((16, 16, 256), f32),
            vmem((4, 16, 16, 256), f32),
        ),
        in_specs=[pl.BlockSpec(memory_space=pltpu.SMEM), hbm, hbm, hbm],
        out_specs=(on_chip, on_chip, on_chip),
        scratch_shapes=[
            cells,
            cells,
            vmem((4, 33, 32, LANES), f32),
            vmem((4, 32, 40, LANES), f32),
            cells,
            cells,
            cells,
            cells,
            vmem((ITERS, 4, 34, 48, LANES), f32),
            vmem((4, 16, 32, LANES), f32),
            vmem((ITERS, 2, 4, 48, LANES), f32),
            vmem((ITERS, 2, 4, 32, LANES), f32),
            vmem((8, 2, 4, 32, LANES), f32),
            vmem((4, 32, LANES), f32),
            vmem((4, 32, LANES), f32),
            vmem((4, 1, 32, LANES), f32),
            vmem((4, 256, LANES), f32),
            vmem((2, 16, 16, LANES), f32),
            vmem((5, 4, 4, 4, 8, LANES), f32),
            *[vmem((16, 4, 8, LANES), f32)] * 5,
            vmem((5, 16, 4, 8, LANES), f32),
            pltpu.SMEM((16,), jnp.int32),
            dma((5, 4)),
            dma((2,)),
            dma((2,)),
            dma((ITERS, 4)),
            dma((ITERS, 4)),
            dma((5, 4)),
            dma((5, 4)),
            dma((5,)),
            dma((5, 16)),
            dma((5, 16)),
            dma((5,)),
        ],
        compiler_params=pltpu.CompilerParams(
            collective_id=0, has_side_effects=True, vmem_limit_bytes=60 << 20
        ),
        name="smooth_and_restrict",
    )(owner_map, right_side, alpha_coef, face_coef)
    arrays = (sol, cres, ccoef)
    return pl.pallas_call(
        write_out,
        out_shape=tuple(jax.ShapeDtypeStruct(x.shape, f32) for x in arrays),
        in_specs=[on_chip] * 3,
        out_specs=(hbm,) * 3,
        scratch_shapes=[dma((6,))],
        compiler_params=pltpu.CompilerParams(vmem_limit_bytes=1 << 20),
        name="write_out",
    )(*arrays)


def solution(mesh):
    return jax.shard_map(
        functools.partial(local, mesh.shape["gy"]),
        mesh=mesh,
        in_specs=(
            P("gx", "gy", None),
            P("gx", "gy", None),
            P(None, "gx", "gy", None),
            P("gy", None),
        ),
        out_specs=(P("gx", "gy", None), P("gx", "gy", None), P(None, "gx", "gy", None)),
        check_vma=False,
    )
```
